32 devices in a mesh: dev: 16 (over z, y, core), rhs: 2 (over x).
Axes of the slice: x: 2, y: 2, z: 4, core: 2. Of those that a mesh axis runs over, the one named last changes fastest.
Arguments:
- top_adj: float32 [16, 32, 16, 256], P('rhs', 'dev'), may hold values from -6 to 6
- level1_adj: float32 [16, 16, 64, 128], P('rhs', 'dev'), may hold values from -6 to 6
- image_offsets: int32 [64, 2], P('rhs'), may hold values from -6 to 6
- image_weights: float32 [64], P('rhs'), may hold values from 0.2 to 1
- incidence: float32 [16, 2], replicated, may hold values from -0.6 to 0.6
- child_list: int32 [16, 4], replicated, may hold values from 0 to 63, as said below
- theta_index_top: int32 [128, 3], replicated, may hold values from 0 to 63
- theta_weight_top: float32 [128, 3], replicated, may hold values from -2.7 to 2.7
- phi_weight_top: float32 [32, 3], replicated, may hold values from -2.7 to 2.7
- theta_index_mid: int32 [64, 3], replicated, may hold values from 0 to 31
- theta_weight_mid: float32 [64, 3], replicated, may hold values from -2.7 to 2.7
- phi_weight_mid: float32 [16, 3], replicated, may hold values from -2.7 to 2.7
Outputs:
- level0_adj: float32 [16, 256, 512], P('rhs', 'dev')
The draws below stay inside these ranges and needn't reach their ends.
Inputs may be any that keep to these rules, and one draw needn't show every extreme that they name: `child_list`: row b holds the middle-level boxes 4 b to 4 b + 3, each once.
All inputs are finite; a program needn't handle non-finite values.
Results may differ from the reference program's by a relative error of at most 0.0003.
Values sent between devices are 32-bit elements; how exact they have to be, the bound alone decides.
No kernel may reach another device: no remote copies, remote signals or barrier semaphores. Data moves between devices by JAX's collectives and lax.ppermute only.
A program may use at most 128 MiB of HBM per device.

```python
import math
import jax
import jax.numpy as jnp
from jax import lax

EXC = 16
NT2 = 128
IMAGES = 64
NT1 = 64
NT0 = 32
NP2 = 32
NP1 = 16
NP0 = 8
NB2 = 16
NB1 = 64


def stencil_rows(key, row_count, column_count):
    centre = jnp.arange(row_count, dtype=jnp.int32)[:, None] // 2 + jnp.arange(3, dtype=jnp.int32)[None, :] - 1
    jitter = jax.random.randint(key, (row_count, 3), -1, 2, dtype=jnp.int32)
    return jnp.clip(centre + jitter, 0, column_count - 1).astype(jnp.int32)


def draw_child_list(key, part):
    box_keys = jax.random.split(jax.random.fold_in(key, 7), NB2)

    def shuffle(single_key):
        return jax.random.permutation(single_key, jnp.arange(4, dtype=jnp.int32))
    orders = jax.vmap(shuffle)(box_keys)
    return (orders + 4 * jnp.arange(NB2, dtype=jnp.int32)[:, None]).astype(jnp.int32)


def draw_theta_index_top(key, part):
    return stencil_rows(jax.random.fold_in(key, 11), NT2, NT1)


def draw_theta_index_mid(key, part):
    return stencil_rows(jax.random.fold_in(key, 13), NT1, NT0)


def set_ends(array, own_key, smallest, largest):
    spot = [jax.random.randint(jax.random.fold_in(own_key, axis), (), 0, length) for axis, length in enumerate(array.shape)]
    widest = array.shape.index(max(array.shape))
    neighbour = spot[:widest] + [(spot[widest] + 1) % array.shape[widest]] + spot[widest + 1:]
    return array.at[tuple(spot)].set(smallest).at[tuple(neighbour)].set(largest)


def shard_levels(rng, shape, shards, least, largest):
    level, own = 1.0, jax.random.fold_in(rng, 6)
    for dim, parts in shards:
        steps = jnp.exp(jax.random.uniform(jax.random.fold_in(own, dim), (parts,), jnp.float32, least / len(shards), largest / len(shards)))
        level = level * jnp.repeat(steps, shape[dim] // parts).reshape([-1 if axis == dim else 1 for axis in range(len(shape))])
    return level


def scatter_about(key, extent, scale, bound, cuts=(), held_as=jnp.bfloat16):
    entries = scale * jax.random.normal(key, extent, jnp.float32)
    if cuts:
        entries = entries * shard_levels(key, extent, cuts, -0.22, 0.18)
    return jnp.clip(entries, -bound, bound).astype(held_as)


def setup_inputs(seed: int = 0) -> dict:
    key_list = jax.random.split(jax.random.key(seed), 13)
    return {
        "top_adj": scatter_about(key_list[0], (EXC, NP2, NB2, 2 * NT2), 1.0, 6.0, ((0, 2), (1, 16)), jnp.float32),
        "level1_adj": scatter_about(key_list[1], (EXC, NP1, NB1, 2 * NT1), 1.0, 6.0, ((0, 2), (1, 16)), jnp.float32),
        "image_offsets": set_ends(jax.random.randint(key_list[2], (IMAGES, 2), -6, 7), jax.random.fold_in(key_list[2], 1), -6, 6).astype(jnp.int32),
        "image_weights": jnp.clip(jnp.exp(math.log(1.0) - 1.609438 * jax.random.uniform(key_list[3], (IMAGES,), jnp.float32) ** shard_levels(key_list[3], (IMAGES,), ((0, 2),), -0.2, 0.2)), 0.2, 1.0),
        "incidence": jnp.clip(jax.random.uniform(key_list[4], (EXC, 2), jnp.float32, -0.6, 0.6), -0.6, 0.6),
        "child_list": draw_child_list(jax.random.fold_in(key_list[12], 71), 0),
        "theta_index_top": draw_theta_index_top(jax.random.fold_in(key_list[12], 71), 0),
        "theta_weight_top": scatter_about(key_list[7], (NT2, 3), 0.45, 2.7, (), jnp.float32),
        "phi_weight_top": scatter_about(key_list[8], (NP2, 3), 0.45, 2.7, (), jnp.float32),
        "theta_index_mid": draw_theta_index_mid(jax.random.fold_in(key_list[12], 71), 0),
        "theta_weight_mid": scatter_about(key_list[10], (NT1, 3), 0.45, 2.7, (), jnp.float32),
        "phi_weight_mid": scatter_about(key_list[11], (NP1, 3), 0.45, 2.7, (), jnp.float32),
    }


PHASE_TOP = 18.85
PHASE_MID = 9.42
LATTICE = 12.57


def directions(theta_count, phi_ids, phi_count):
    theta = (math.pi / theta_count) * (jnp.arange(theta_count, dtype=jnp.float32) + 0.5)
    azimuth = (2.0 * math.pi / phi_count) * phi_ids.astype(jnp.float32)
    sin_theta = jnp.sin(theta)
    along_x = jnp.cos(azimuth)[:, None] * sin_theta[None, :]
    along_y = jnp.sin(azimuth)[:, None] * sin_theta[None, :]
    along_z = jnp.cos(theta)
    return along_x, along_y, along_z


def theta_matrix(index, weight, columns):
    hits = (index[:, :, None] == jnp.arange(columns, dtype=jnp.int32)[None, None, :]).astype(jnp.float32)
    return jnp.sum(weight[:, :, None] * hits, axis=1)


def phi_matrix(weight, row_ids, coarse_count, column_ids):
    target = (row_ids[:, None] // 2 + jnp.arange(3, dtype=jnp.int32)[None, :] - 1) % coarse_count
    hits = (target[:, :, None] == column_ids[None, None, :]).astype(jnp.float32)
    return jnp.sum(weight[:, :, None] * hits, axis=1)


def octant_phase(factor, octant, along_x, along_y, along_z):
    sign_x = 2.0 * (octant % 2) - 1.0
    sign_y = 2.0 * (octant // 2) - 1.0
    angle = factor * (sign_x * along_x + sign_y * along_y - along_z[None, :])
    return jnp.cos(angle), jnp.sin(angle)


def lattice_sum(offsets, weighted, incident, along_x, along_y):
    phase_arg = LATTICE * (
        offsets[:, 0, None, None, None] * (along_x[None, None] - incident[None, :, 0, None, None])
        + offsets[:, 1, None, None, None] * (along_y[None, None] - incident[None, :, 1, None, None]))
    sum_real = jnp.sum(weighted[:, None, None, None] * jnp.cos(phase_arg), axis=0)
    sum_imag = jnp.sum(weighted[:, None, None, None] * jnp.sin(phase_arg), axis=0)
    return sum_real, sum_imag


def upper_level(top_real, top_imag, along_x, along_y, along_z, theta_map, phi_map, children, top_ids):
    summed = None
    for octant in range(4):
        cosine, sine = octant_phase(PHASE_TOP, octant, along_x, along_y, along_z)
        cosine = cosine[:, None, :]
        sine = sine[:, None, :]
        stacked = jnp.stack([top_real * cosine - top_imag * sine, top_real * sine + top_imag * cosine])
        theta_done = jnp.einsum("...pbt,tu->...pbu", stacked, theta_map, precision=lax.Precision.HIGHEST)
        phi_done = jnp.einsum("...pbu,pq->...qbu", theta_done, phi_map, precision=lax.Precision.HIGHEST)
        select_map = (children[:, octant][:, None] - 4 * top_ids[:, None]
                      == jnp.arange(4, dtype=jnp.int32)[None, :]).astype(jnp.float32)
        placed = phi_done[..., None, :] * select_map[:, :, None]
        summed = placed if summed is None else summed + placed
    merged = summed.reshape(summed.shape[:-3] + (summed.shape[-3] * 4, summed.shape[-1]))
    return jnp.concatenate([merged[0], merged[1]], axis=-1)


def lower_level(middle, along_x, along_y, along_z, theta_map, phi_map):
    half_width = middle.shape[-1] // 2
    mid_real = middle[..., :half_width]
    mid_imag = middle[..., half_width:]
    real_parts = []
    imag_parts = []
    for octant in range(4):
        cosine, sine = octant_phase(PHASE_MID, octant, along_x, along_y, along_z)
        cosine = cosine[:, None, :]
        sine = sine[:, None, :]
        real_parts.append(mid_real * cosine - mid_imag * sine)
        imag_parts.append(mid_real * sine + mid_imag * cosine)
    stacked = jnp.stack([jnp.stack(real_parts, axis=-2), jnp.stack(imag_parts, axis=-2)])
    theta_done = jnp.einsum("...pijt,tu->...piju", stacked, theta_map, precision=lax.Precision.HIGHEST)
    phi_done = jnp.einsum("c...piju,pq->...ijqcu", theta_done, phi_map, precision=lax.Precision.HIGHEST)
    result_shape = phi_done.shape
    return phi_done.reshape(result_shape[:-5] + (result_shape[-5] * 4, result_shape[-3] * result_shape[-2] * result_shape[-1]))


def reference(top_adj, level1_adj, image_offsets, image_weights, incidence, child_list,
              theta_index_top, theta_weight_top, phi_weight_top, theta_index_mid, theta_weight_mid, phi_weight_mid):
    top_phi = jnp.arange(NP2, dtype=jnp.int32)
    top_x, top_y, top_z = directions(NT2, top_phi, NP2)
    mid_phi = jnp.arange(NP1, dtype=jnp.int32)
    mid_x, mid_y, mid_z = directions(NT1, mid_phi, NP1)
    theta_top = theta_matrix(theta_index_top, theta_weight_top, NT1)
    phi_top = phi_matrix(phi_weight_top, top_phi, NP1, mid_phi)
    theta_mid = theta_matrix(theta_index_mid, theta_weight_mid, NT0)
    phi_mid = phi_matrix(phi_weight_mid, mid_phi, NP0, jnp.arange(NP0, dtype=jnp.int32))
    offsets = image_offsets.astype(jnp.float32)
    weighted = image_weights * (float(IMAGES) ** -0.5)
    top_ids = jnp.arange(NB2, dtype=jnp.int32)

    def single(inputs):
        top_pattern, mid_pattern, incident = inputs
        sum_real, sum_imag = lattice_sum(offsets, weighted, incident[None, :], top_x, top_y)
        sum_real = sum_real[0][:, None, :]
        sum_imag = sum_imag[0][:, None, :]
        top_real = top_pattern[..., :NT2]
        top_imag = top_pattern[..., NT2:]
        shifted_real = sum_real * top_real + sum_imag * top_imag
        shifted_imag = sum_real * top_imag - sum_imag * top_real
        above = upper_level(shifted_real, shifted_imag, top_x, top_y, top_z, theta_top, phi_top, child_list, top_ids)
        return lower_level(mid_pattern + above, mid_x, mid_y, mid_z, theta_mid, phi_mid)

    return lax.map(single, (top_adj, level1_adj, incidence))
```

```python
import math

import jax
import jax.numpy as jnp
from jax import lax
from jax.experimental import pallas as pl
from jax.experimental.pallas import tpu as pltpu
from jax.sharding import PartitionSpec as P

PHASE_TOP = 18.85
PHASE_MID = 9.42
LATTICE = 12.57
LANES = 128
HIGHEST = lax.Precision.HIGHEST
VMEM = pl.BlockSpec(memory_space=pltpu.VMEM)
SMEM = pl.BlockSpec(memory_space=pltpu.SMEM)


def sincos(x):
    n = jnp.floor(x * (2.0 / math.pi) + 0.5)
    r = x - n * 1.5703125
    r = r - n * 4.837512969970703125e-4
    r = r - n * 7.54978995489188216e-8
    z = r * r
    s = r + r * z * (-1.6666654611e-1 + z * (8.3321608736e-3 - z * 1.9515295891e-4))
    c = (1.0 - 0.5 * z) + z * z * (
        4.166664568298827e-2 + z * (-1.388731625493765e-3 + z * 2.443315711809948e-5)
    )
    quadrant = n.astype(jnp.int32)
    swap = (quadrant & 1) == 1
    sine = jnp.where(swap, c, s)
    cosine = jnp.where(swap, s, c)
    sine = jnp.where((quadrant & 2) == 2, -sine, sine)
    cosine = jnp.where(((quadrant + 1) & 2) == 2, -cosine, cosine)
    return sine, cosine


def directions(shape, theta_count, phi_count, row0=0):
    rows = lax.broadcasted_iota(jnp.int32, shape, 0).astype(jnp.float32) + row0
    cols = lax.broadcasted_iota(jnp.int32, shape, 1)
    theta = math.pi / theta_count * ((cols % theta_count).astype(jnp.float32) + 0.5)
    sin_theta, cos_theta = sincos(theta)
    sin_phi, cos_phi = sincos(2.0 * math.pi / phi_count * rows)
    return cos_phi * sin_theta, sin_phi * sin_theta, cos_theta


def cmul(ar, ai, br, bi):
    return ar * br - ai * bi, ar * bi + ai * br


def loop(count, body):
    if count <= 16:
        for step in range(count):
            body(step)
    else:
        lax.fori_loop(0, count, lambda step, carry: (body(step), carry)[1], 0)


def pack_kernel(dests, per_dest, re_ref, im_ref, l_ref, o_ref):
    exc, phi_local, boxes, _ = re_ref.shape
    mids = l_ref.shape[2]
    mid_phi = l_ref.shape[1]
    a_rows = [ref.reshape(exc * phi_local * boxes, LANES) for ref in (re_ref, im_ref)]
    l_rows = l_ref.reshape(exc * mid_phi * mids, LANES)
    for dest in range(dests):
        tile = 0
        for phi in range(phi_local):
            for box in range(per_dest):
                row = phi * boxes + dest * per_dest + box
                for part in range(2):
                    o_ref[dest, tile] = a_rows[part][pl.ds(row, exc, stride=phi_local * boxes), :]
                    tile += 1
        for phi in range(mid_phi):
            for mid in range(4 * per_dest):
                row = phi * mids + dest * 4 * per_dest + mid
                o_ref[dest, tile] = l_rows[pl.ds(row, exc, stride=mid_phi * mids), :]
                tile += 1


def pack(top_adj, level1_adj, dev_count):
    exc, phi_local, boxes, width = top_adj.shape
    mid_phi, mids = level1_adj.shape[1:3]
    per_dest = boxes // dev_count
    block = 8
    dests = block // per_dest
    tiles = phi_local * per_dest * (width // LANES) + mid_phi * 4 * per_dest
    return pl.pallas_call(
        lambda *refs: pack_kernel(dests, per_dest, *refs),
        grid=(boxes // block,),
        in_specs=[
            pl.BlockSpec((exc, phi_local, block, LANES), lambda g: (0, 0, g, 0)),
            pl.BlockSpec((exc, phi_local, block, LANES), lambda g: (0, 0, g, 1)),
            pl.BlockSpec((exc, mid_phi, 4 * block, LANES), lambda g: (0, 0, g, 0)),
        ],
        out_specs=pl.BlockSpec((dests, tiles, exc, LANES), lambda g: (g, 0, 0, 0)),
        out_shape=jax.ShapeDtypeStruct((dev_count, tiles, exc, LANES), jnp.float32),
        compiler_params=pltpu.CompilerParams(vmem_limit_bytes=8 << 20),
        name="pack",
    )(top_adj, top_adj, level1_adj)


def theta_block(index_ref, weight_ref, columns):
    samples = index_ref.shape[1]
    rows = lax.broadcasted_iota(jnp.int32, (columns, samples), 0)
    total = jnp.zeros((columns, samples), jnp.float32)
    for s in range(3):
        hit = rows == index_ref[s : s + 1, :]
        total = total + jnp.where(hit, weight_ref[s : s + 1, :], 0.0)
    return total


def coef_kernel(
    sizes,
    where_ref,
    inc_ref,
    child_ref,
    phi_top_ref,
    phi_mid_ref,
    img_ref,
    index_top_ref,
    weight_top_ref,
    index_mid_ref,
    weight_mid_ref,
    w_ref,
    pw2_ref,
    pw1_ref,
    m2_ref,
    m1_ref,
    tc_ref,
    ts_ref,
    dir_ref,
    ph_ref,
    ob_ref,
):
    exc, np2, np1, nt2, images, per_dev = sizes
    nt1, nt0 = nt2 // 2, nt2 // 4
    half = np2 // 2
    first_box = where_ref[0] * per_dev
    first_exc = where_ref[1] * exc

    def splat_top(p):
        for s in range(3):
            pw2_ref[p * 3 + s] = jnp.full((exc, LANES), phi_top_ref[s, p], jnp.float32)

    def splat_mid(p):
        for s in range(3):
            pw1_ref[p * 3 + s] = jnp.full((exc, LANES), phi_mid_ref[s, p], jnp.float32)

    loop(np2, splat_top)
    loop(np1, splat_mid)

    m2_ref[...] = jnp.zeros(m2_ref.shape, jnp.float32)
    m1_ref[...] = jnp.zeros(m1_ref.shape, jnp.float32)
    theta_top = theta_block(index_top_ref, weight_top_ref, nt1)
    theta_mid = theta_block(index_mid_ref, weight_mid_ref, nt0)
    for part in range(2):
        m2_ref[part * nt1 : (part + 1) * nt1, part * nt2 : (part + 1) * nt2] = theta_top
    for part in range(4):
        m1_ref[part * nt0 : (part + 1) * nt0, part * nt1 : (part + 1) * nt1] = theta_mid

    mx, my, mz = directions((np1, LANES), nt1, np1)
    sxs, sxc = sincos(PHASE_MID * mx)
    sys_, syc = sincos(PHASE_MID * my)
    szs, szc = sincos(PHASE_MID * mz)
    lane = lax.broadcasted_iota(jnp.int32, (np1, LANES), 1)
    sign = jnp.where(lane < nt1, -1.0, 1.0)
    for octant in range(4):
        fx = 2.0 * (octant % 2) - 1.0
        fy = 2.0 * (octant // 2) - 1.0
        re, im = cmul(sxc, fx * sxs, syc, fy * sys_)
        re, im = cmul(re, im, szc, -szs)
        tc_ref[octant * np1 : (octant + 1) * np1, :] = re
        ts_ref[octant * np1 : (octant + 1) * np1, :] = im * sign

    ux, uy, uz = directions((np2, LANES), nt2, np2)
    dir_ref[0] = ux
    dir_ref[1] = uy
    axs, axc = sincos(PHASE_TOP * ux)
    ays, ayc = sincos(PHASE_TOP * uy)
    azs, azc = sincos(PHASE_TOP * uz)
    for box in range(per_dev):
        for slot in range(4):
            fx = jnp.float32(0.0)
            fy = jnp.float32(0.0)
            for octant in range(4):
                hit = child_ref[first_box + box, octant] == 4 * (first_box + box) + slot
                fx = fx + jnp.where(hit, jnp.float32(2.0 * (octant % 2) - 1.0), jnp.float32(0.0))
                fy = fy + jnp.where(hit, jnp.float32(2.0 * (octant // 2) - 1.0), jnp.float32(0.0))
            re, im = cmul(axc, fx * axs, ayc, fy * ays)
            re, im = cmul(re, im, azc, -azs)
            ph_ref[box * 8 + slot * 2] = re
            ph_ref[box * 8 + slot * 2 + 1] = im

    image = img_ref[...]
    ox, oy, wt = image[0:1, :], image[1:2, :], image[2:3, :]
    excs = lax.broadcasted_iota(jnp.int32, (exc, LANES), 0)
    kx = jnp.zeros((exc, LANES), jnp.float32)
    ky = jnp.zeros((exc, LANES), jnp.float32)
    for e in range(exc):
        kx = jnp.where(excs == e, inc_ref[0, first_exc + e], kx)
        ky = jnp.where(excs == e, inc_ref[1, first_exc + e], ky)
    fs, fc = sincos(LATTICE * (ox * kx + oy * ky))
    wc = (wt * fc)[:, :images]
    ws = (wt * fs)[:, :images]
    left_c = jnp.concatenate([wc, -ws, wc, -ws], axis=0)
    left_s = jnp.concatenate([ws, wc, -ws, -wc], axis=0)
    ob_ref[0] = jnp.transpose(jnp.broadcast_to(LATTICE * ox, (LANES, LANES)))[:images]
    ob_ref[1] = jnp.transpose(jnp.broadcast_to(LATTICE * oy, (LANES, LANES)))[:images]

    def lattice(p):
        ux_row = dir_ref[0, pl.ds(p, 1), :]
        uy_row = dir_ref[1, pl.ds(p, 1), :]
        sb, cb = sincos(ob_ref[0] * ux_row + ob_ref[1] * uy_row)
        total = jnp.dot(
            left_c, cb, precision=HIGHEST, preferred_element_type=jnp.float32
        ) + jnp.dot(left_s, sb, precision=HIGHEST, preferred_element_type=jnp.float32)
        for mirror in range(2):
            sr = total[(2 * mirror) * exc : (2 * mirror + 1) * exc]
            si = total[(2 * mirror + 1) * exc : (2 * mirror + 2) * exc]
            q = p + mirror * half
            for tile in range(4 * per_dev):
                pr = ph_ref[2 * tile, pl.ds(q, 1), :]
                pi = ph_ref[2 * tile + 1, pl.ds(q, 1), :]
                re, im = cmul(pr, pi, sr, -si)
                w_ref[q, 2 * tile] = re
                w_ref[q, 2 * tile + 1] = im

    loop(half, lattice)


def coefficients(where, inc, child, phi_top, phi_mid, img, tit, twt, tim, twm, exc, nt2, images):
    np2, np1 = phi_top.shape[1], phi_mid.shape[1]
    nt1 = nt2 // 2
    per_dev = images[1]
    sizes = (exc, np2, np1, nt2, images[0], per_dev)
    f32 = jnp.float32
    return pl.pallas_call(
        lambda *refs: coef_kernel(sizes, *refs),
        in_specs=[SMEM] * 5 + [VMEM] * 5,
        out_specs=[VMEM] * 7,
        out_shape=[
            jax.ShapeDtypeStruct((np2, 8 * per_dev, exc, LANES), f32),
            jax.ShapeDtypeStruct((np2 * 3, exc, LANES), f32),
            jax.ShapeDtypeStruct((np1 * 3, exc, LANES), f32),
            jax.ShapeDtypeStruct((LANES, 2 * nt2), f32),
            jax.ShapeDtypeStruct((LANES, 4 * nt1), f32),
            jax.ShapeDtypeStruct((4 * np1, LANES), f32),
            jax.ShapeDtypeStruct((4 * np1, LANES), f32),
        ],
        scratch_shapes=[
            pltpu.VMEM((2, np2, LANES), f32),
            pltpu.VMEM((8 * per_dev, np2, LANES), f32),
            pltpu.VMEM((2, images[0], LANES), f32),
        ],
        compiler_params=pltpu.CompilerParams(vmem_limit_bytes=32 << 20),
        name="coefficients",
    )(where, inc, child, phi_top, phi_mid, img, tit, twt, tim, twm)


def phi_pass(count, contribution, emit):
    first = contribution(count - 1)
    second = contribution(0)
    carry = [x + y for x, y in zip(first[2], second[1])], list(second[2])

    def step(q, carry):
        here, after = carry
        new = contribution((q + 1) % count if isinstance(q, int) else lax.rem(q + 1, count))
        emit(q, [x + y for x, y in zip(here, new[0])])
        return [x + y for x, y in zip(after, new[1])], list(new[2])

    if count <= 16:
        for q in range(count):
            carry = step(q, carry)
    else:
        lax.fori_loop(0, count, step, carry)


def main_kernel(
    sizes,
    r_ref,
    w_ref,
    pw2_ref,
    pw1_ref,
    m2_ref,
    m1_ref,
    tc_ref,
    ts_ref,
    o_ref,
    x_ref,
    g_ref,
    h_ref,
    y_ref,
    z_ref,
):
    exc, np2, np1, nt2, phi_local, per_dev = sizes
    np0 = np1 // 2
    mid_local = phi_local // 2
    base = phi_local * per_dev * 2
    mids = 4 * per_dev
    nt = (((1,), (1,)), ((), ()))

    for box in range(per_dev):

        def top(m, box=box):
            out = [[None] * 8 for _ in range(3)]
            for parity in range(2):
                p = 2 * m + parity
                tile = ((p % phi_local) * per_dev + box) * 2
                ar = r_ref[p // phi_local, tile]
                ai = r_ref[p // phi_local, tile + 1]
                weights = [pw2_ref[3 * p + s] for s in range(3)]
                for slot in range(4):
                    wr = w_ref[p, box * 8 + slot * 2]
                    wi = w_ref[p, box * 8 + slot * 2 + 1]
                    for c, value in enumerate(cmul(ar, ai, wr, wi)):
                        for s in range(3):
                            term = weights[s] * value
                            k = slot * 2 + c
                            out[s][k] = term if out[s][k] is None else out[s][k] + term
            return out

        def keep(q, values):
            for slot in range(4):
                for c in range(2):
                    x_ref[
                        pl.ds((q * 4 + slot) * exc, exc), c * LANES : (c + 1) * LANES
                    ] = values[slot * 2 + c]

        phi_pass(np1, top, keep)
        rows = x_ref.shape[0]
        block = min(rows, 512)

        def theta(part, box=box):
            done = lax.dot_general(
                x_ref[pl.ds(part * block, block), :],
                m2_ref[...],
                nt,
                precision=HIGHEST,
                preferred_element_type=jnp.float32,
            )
            per_block = block // (4 * exc)
            for n in range(per_block):
                q = part * per_block + n
                for slot in range(4):
                    row = (n * 4 + slot) * exc
                    mid = box * 4 + slot
                    value = (
                        done[row : row + exc]
                        + r_ref[q // mid_local, base + (q % mid_local) * mids + mid]
                    )
                    g_ref[q, mid] = value
                    h_ref[q, mid] = pltpu.roll(value, LANES // 2, 1)

        loop(rows // block, theta)

    o_rows = o_ref.reshape(exc * 4 * mids, o_ref.shape[2])

    for octant in range(4):
        for box in range(per_dev):

            def middle(m, octant=octant, box=box):
                out = [[None] * 4 for _ in range(3)]
                for parity in range(2):
                    q = 2 * m + parity
                    cosine = tc_ref[pl.ds(octant * np1 + q, 1), :]
                    sine = ts_ref[pl.ds(octant * np1 + q, 1), :]
                    weights = [pw1_ref[3 * q + s] for s in range(3)]
                    for slot in range(4):
                        value = (
                            g_ref[q, box * 4 + slot] * cosine + h_ref[q, box * 4 + slot] * sine
                        )
                        for s in range(3):
                            term = weights[s] * value
                            out[s][slot] = term if out[s][slot] is None else out[s][slot] + term
                return out

            def keep_low(q, values, octant=octant, box=box):
                for slot in range(4):
                    k = (box * 4 + slot) * 4 + octant
                    y_ref[q // 2, pl.ds(k * exc, exc), pl.ds((q % 2) * LANES, LANES)] = values[
                        slot
                    ]

            phi_pass(np0, middle, keep_low)

    def finish(pair):
        done = lax.dot_general(
            y_ref[pair],
            m1_ref[...],
            nt,
            precision=HIGHEST,
            preferred_element_type=jnp.float32,
        )
        start = pair * LANES
        lanes = pl.ds(start if isinstance(pair, int) else pl.multiple_of(start, LANES), LANES)
        for k in range(4 * mids):
            z_ref[pl.ds(k, exc, stride=4 * mids), :] = done[k * exc : (k + 1) * exc]
        o_rows[:, lanes] = z_ref[...]

    loop(np0 // 2, finish)


def main(received, coefs, exc, np2, np1, nt2, phi_local, per_dev):
    mids = 4 * per_dev
    np0 = np1 // 2
    f32 = jnp.float32
    sizes = (exc, np2, np1, nt2, phi_local, per_dev)
    return pl.pallas_call(
        lambda *refs: main_kernel(sizes, *refs),
        in_specs=[VMEM] * 8,
        out_specs=VMEM,
        out_shape=jax.ShapeDtypeStruct((exc, 4 * mids, np0 * (nt2 // 2)), f32),
        scratch_shapes=[
            pltpu.VMEM((np1 * 4 * exc, 2 * LANES), f32),
            pltpu.VMEM((np1, mids, exc, LANES), f32),
            pltpu.VMEM((np1, mids, exc, LANES), f32),
            pltpu.VMEM((np0 // 2, 4 * mids * exc, 2 * LANES), f32),
            pltpu.VMEM((4 * mids * exc, LANES), f32),
        ],
        compiler_params=pltpu.CompilerParams(vmem_limit_bytes=56 << 20),
        name="levels",
    )(received, *coefs)


def local(
    top_adj,
    level1_adj,
    image_offsets,
    image_weights,
    incidence,
    child_list,
    theta_index_top,
    theta_weight_top,
    phi_weight_top,
    theta_index_mid,
    theta_weight_mid,
    phi_weight_mid,
):
    dev_count = lax.axis_size("dev")
    rhs_count = lax.axis_size("rhs")
    exc, phi_local, top_boxes, top_width = top_adj.shape
    per_dev = top_boxes // dev_count
    nt2 = top_width // 2
    np2 = phi_local * dev_count
    np1 = np2 // 2
    images = image_offsets.shape[0] * rhs_count

    packed = pack(top_adj, level1_adj, dev_count)
    received = lax.all_to_all(packed, "dev", split_axis=0, concat_axis=0, tiled=True)

    own = jnp.concatenate(
        [
            image_offsets.T.astype(jnp.float32),
            image_weights[None] * float(images) ** (-0.5),
        ],
        axis=0,
    )
    parts = [own]
    for shift in range(1, rhs_count):
        parts.append(
            lax.ppermute(own, "rhs", [(i, (i + shift) % rhs_count) for i in range(rhs_count)])
        )
    img = jnp.concatenate(parts + [jnp.zeros((3, LANES - images), jnp.float32)], axis=1)
    where = jnp.stack([lax.axis_index("dev"), lax.axis_index("rhs")]).astype(jnp.int32)
    coefs = coefficients(
        where,
        incidence.T,
        child_list,
        phi_weight_top.T,
        phi_weight_mid.T,
        img,
        theta_index_top.T,
        theta_weight_top.T,
        theta_index_mid.T,
        theta_weight_mid.T,
        exc,
        nt2,
        (images, per_dev),
    )
    return main(received, coefs, exc, np2, np1, nt2, phi_local, per_dev)


def solution(mesh):
    placed = (
        P("rhs", "dev", None, None),
        P("rhs", "dev", None, None),
        P("rhs", None),
        P("rhs"),
        P(),
        P(),
        P(),
        P(),
        P(),
        P(),
        P(),
        P(),
    )
    return jax.shard_map(
        local, mesh=mesh, in_specs=placed, out_specs=P("rhs", "dev", None), check_vma=False
    )
```

```python
import math

import jax
import jax.numpy as jnp
from jax import lax
from jax.experimental import pallas as pl
from jax.experimental.pallas import tpu as pltpu
from jax.sharding import PartitionSpec as P

PHASE_TOP = 18.85
PHASE_MID = 9.42
LATTICE = 12.57
LANES = 128
HIGHEST = lax.Precision.HIGHEST
VMEM = pl.BlockSpec(memory_space=pltpu.VMEM)
SMEM = pl.BlockSpec(memory_space=pltpu.SMEM)


def sincos(x):
    n = jnp.floor(x * (2.0 / math.pi) + 0.5)
    r = x - n * 1.5703125
    r = r - n * 4.837512969970703125e-4
    r = r - n * 7.54978995489188216e-8
    z = r * r
    s = r + r * z * (-1.6666654611e-1 + z * (8.3321608736e-3 - z * 1.9515295891e-4))
    c = (1.0 - 0.5 * z) + z * z * (
        4.166664568298827e-2 + z * (-1.388731625493765e-3 + z * 2.443315711809948e-5)
    )
    quadrant = n.astype(jnp.int32)
    swap = (quadrant & 1) == 1
    sine = jnp.where(swap, c, s)
    cosine = jnp.where(swap, s, c)
    sine = jnp.where((quadrant & 2) == 2, -sine, sine)
    cosine = jnp.where(((quadrant + 1) & 2) == 2, -cosine, cosine)
    return sine, cosine


def directions(shape, theta_count, phi_count, row0=0):
    rows = lax.broadcasted_iota(jnp.int32, shape, 0).astype(jnp.float32) + row0
    cols = lax.broadcasted_iota(jnp.int32, shape, 1)
    theta = math.pi / theta_count * ((cols % theta_count).astype(jnp.float32) + 0.5)
    sin_theta, cos_theta = sincos(theta)
    sin_phi, cos_phi = sincos(2.0 * math.pi / phi_count * rows)
    return cos_phi * sin_theta, sin_phi * sin_theta, cos_theta


def cmul(ar, ai, br, bi):
    return ar * br - ai * bi, ar * bi + ai * br


def loop(count, body):
    if count <= 16:
        for step in range(count):
            body(step)
    else:
        lax.fori_loop(0, count, lambda step, carry: (body(step), carry)[1], 0)


def pack_kernel(per_dest, a_hbm, l_hbm, o_hbm, re_ref, im_ref, mid_ref, top_out, mid_out, sems):
    exc, phi_local, boxes, _ = re_ref.shape
    mid_phi, mids = mid_ref.shape[1:3]
    copies = [
        pltpu.make_async_copy(a_hbm.at[:, :, :, pl.ds(0, LANES)], re_ref, sems.at[0]),
        pltpu.make_async_copy(a_hbm.at[:, :, :, pl.ds(LANES, LANES)], im_ref, sems.at[1]),
        pltpu.make_async_copy(l_hbm, mid_ref, sems.at[2]),
    ]
    for copy in copies:
        copy.start()
    top_tiles = top_out.shape[1]
    mid_tiles = mid_out.shape[1]

    for part, ref in enumerate((re_ref, im_ref)):
        rows = ref.reshape(exc * phi_local * boxes, LANES)
        copies[part].wait()

        def top(dest, rows=rows, part=part):
            for phi in range(phi_local):
                for box in range(per_dest):
                    row = phi * boxes + dest * per_dest + box
                    tile = (phi * per_dest + box) * 2 + part
                    top_out[dest, tile] = rows[pl.ds(row, exc, stride=phi_local * boxes), :]

        loop(boxes // per_dest, top)

    leave = [
        pltpu.make_async_copy(top_out, o_hbm.at[:, pl.ds(0, top_tiles)], sems.at[3]),
        pltpu.make_async_copy(mid_out, o_hbm.at[:, pl.ds(top_tiles, mid_tiles)], sems.at[4]),
    ]
    leave[0].start()
    mid_rows = mid_ref.reshape(exc * mid_phi * mids, LANES)
    copies[2].wait()

    def middle(dest):
        for phi in range(mid_phi):
            for mid in range(4 * per_dest):
                row = phi * mids + dest * 4 * per_dest + mid
                tile = phi * 4 * per_dest + mid
                mid_out[dest, tile] = mid_rows[pl.ds(row, exc, stride=mid_phi * mids), :]

    loop(boxes // per_dest, middle)
    leave[1].start()
    for copy in leave:
        copy.wait()


def pack(top_adj, level1_adj, dev_count):
    exc, phi_local, boxes, _ = top_adj.shape
    mid_phi, mids = level1_adj.shape[1:3]
    per_dest = boxes // dev_count
    top_tiles = phi_local * per_dest * 2
    mid_tiles = mid_phi * 4 * per_dest
    f32 = jnp.float32
    hbm = pl.BlockSpec(memory_space=pltpu.HBM)
    return pl.pallas_call(
        lambda *refs: pack_kernel(per_dest, *refs),
        in_specs=[hbm] * 2,
        out_specs=hbm,
        out_shape=jax.ShapeDtypeStruct((dev_count, top_tiles + mid_tiles, exc, LANES), f32),
        scratch_shapes=[
            pltpu.VMEM((exc, phi_local, boxes, LANES), f32),
            pltpu.VMEM((exc, phi_local, boxes, LANES), f32),
            pltpu.VMEM((exc, mid_phi, mids, LANES), f32),
            pltpu.VMEM((dev_count, top_tiles, exc, LANES), f32),
            pltpu.VMEM((dev_count, mid_tiles, exc, LANES), f32),
            pltpu.SemaphoreType.DMA((5,)),
        ],
        compiler_params=pltpu.CompilerParams(vmem_limit_bytes=67043328),
        name="pack",
    )(top_adj, level1_adj)


def theta_block(index_ref, weight_ref, columns):
    samples = index_ref.shape[1]
    rows = lax.broadcasted_iota(jnp.int32, (columns, samples), 0)
    total = jnp.zeros((columns, samples), jnp.float32)
    for s in range(3):
        hit = rows == index_ref[s : s + 1, :]
        total = total + jnp.where(hit, weight_ref[s : s + 1, :], 0.0)
    return total


def coef_kernel(
    sizes,
    where_ref,
    inc_ref,
    child_ref,
    phi_top_ref,
    phi_mid_ref,
    img_ref,
    index_top_ref,
    weight_top_ref,
    index_mid_ref,
    weight_mid_ref,
    w_ref,
    pw2_ref,
    pw1_ref,
    m2_ref,
    m1_ref,
    tc_ref,
    ts_ref,
    dir_ref,
    ph_ref,
    ob_ref,
    fm_ref,
):
    exc, np2, np1, nt2, images, per_dev = sizes
    nt1, nt0 = nt2 // 2, nt2 // 4
    half = np2 // 2
    first_box = where_ref[0] * per_dev
    first_exc = where_ref[1] * exc

    def splat_top(p):
        for s in range(3):
            pw2_ref[p * 3 + s] = jnp.full((exc, LANES), phi_top_ref[s, p], jnp.float32)

    def splat_mid(p):
        for s in range(3):
            pw1_ref[p * 3 + s] = jnp.full((exc, LANES), phi_mid_ref[s, p], jnp.float32)

    loop(np2, splat_top)
    loop(np1, splat_mid)

    theta_top = theta_block(index_top_ref, weight_top_ref, nt1)
    theta_mid = theta_block(index_mid_ref, weight_mid_ref, nt0)
    for parts, block, m_ref in ((2, theta_top, m2_ref), (4, theta_mid, m1_ref)):
        high, width = block.shape
        fm_ref[...] = jnp.zeros(fm_ref.shape, jnp.float32)
        for part in range(parts):
            fm_ref[part * high : (part + 1) * high, part * width : (part + 1) * width] = block
        full = jnp.transpose(fm_ref[...])
        coarse = full.astype(jnp.bfloat16)
        m_ref[:, :LANES] = coarse
        m_ref[:, LANES:] = (full - coarse.astype(jnp.float32)).astype(jnp.bfloat16)

    mx, my, mz = directions((np1, LANES), nt1, np1)
    sxs, sxc = sincos(PHASE_MID * mx)
    sys_, syc = sincos(PHASE_MID * my)
    szs, szc = sincos(PHASE_MID * mz)
    lane = lax.broadcasted_iota(jnp.int32, (np1, LANES), 1)
    sign = jnp.where(lane < nt1, -1.0, 1.0)
    for octant in range(4):
        fx = 2.0 * (octant % 2) - 1.0
        fy = 2.0 * (octant // 2) - 1.0
        re, im = cmul(sxc, fx * sxs, syc, fy * sys_)
        re, im = cmul(re, im, szc, -szs)
        tc_ref[octant * np1 : (octant + 1) * np1, :] = re
        ts_ref[octant * np1 : (octant + 1) * np1, :] = im * sign

    ux, uy, uz = directions((np2, LANES), nt2, np2)
    dir_ref[0] = ux
    dir_ref[1] = uy
    axs, axc = sincos(PHASE_TOP * ux)
    ays, ayc = sincos(PHASE_TOP * uy)
    azs, azc = sincos(PHASE_TOP * uz)
    for box in range(per_dev):
        for slot in range(4):
            fx = jnp.float32(0.0)
            fy = jnp.float32(0.0)
            for octant in range(4):
                hit = child_ref[first_box + box, octant] == 4 * (first_box + box) + slot
                fx = fx + jnp.where(hit, jnp.float32(2.0 * (octant % 2) - 1.0), jnp.float32(0.0))
                fy = fy + jnp.where(hit, jnp.float32(2.0 * (octant // 2) - 1.0), jnp.float32(0.0))
            re, im = cmul(axc, fx * axs, ayc, fy * ays)
            re, im = cmul(re, im, azc, -azs)
            ph_ref[box * 8 + slot * 2] = re
            ph_ref[box * 8 + slot * 2 + 1] = im

    image = img_ref[...]
    ox, oy, wt = image[0:1, :], image[1:2, :], image[2:3, :]
    excs = lax.broadcasted_iota(jnp.int32, (exc, LANES), 0)
    kx = jnp.zeros((exc, LANES), jnp.float32)
    ky = jnp.zeros((exc, LANES), jnp.float32)
    for e in range(exc):
        kx = jnp.where(excs == e, inc_ref[0, first_exc + e], kx)
        ky = jnp.where(excs == e, inc_ref[1, first_exc + e], ky)
    fs, fc = sincos(LATTICE * (ox * kx + oy * ky))
    wc = (wt * fc)[:, :images]
    ws = (wt * fs)[:, :images]
    left_c = jnp.concatenate([wc, -ws, wc, -ws], axis=0)
    left_s = jnp.concatenate([ws, wc, -ws, -wc], axis=0)
    ob_ref[0] = jnp.transpose(jnp.broadcast_to(LATTICE * ox, (LANES, LANES)))[:images]
    ob_ref[1] = jnp.transpose(jnp.broadcast_to(LATTICE * oy, (LANES, LANES)))[:images]

    def lattice(p):
        ux_row = dir_ref[0, pl.ds(p, 1), :]
        uy_row = dir_ref[1, pl.ds(p, 1), :]
        sb, cb = sincos(ob_ref[0] * ux_row + ob_ref[1] * uy_row)
        total = jnp.dot(
            left_c, cb, precision=HIGHEST, preferred_element_type=jnp.float32
        ) + jnp.dot(left_s, sb, precision=HIGHEST, preferred_element_type=jnp.float32)
        for mirror in range(2):
            sr = total[(2 * mirror) * exc : (2 * mirror + 1) * exc]
            si = total[(2 * mirror + 1) * exc : (2 * mirror + 2) * exc]
            q = p + mirror * half
            for tile in range(4 * per_dev):
                pr = ph_ref[2 * tile, pl.ds(q, 1), :]
                pi = ph_ref[2 * tile + 1, pl.ds(q, 1), :]
                re, im = cmul(pr, pi, sr, -si)
                w_ref[q, 2 * tile] = re
                w_ref[q, 2 * tile + 1] = im

    loop(half, lattice)


def coefficients(where, inc, child, phi_top, phi_mid, img, tit, twt, tim, twm, exc, nt2, images):
    np2, np1 = phi_top.shape[1], phi_mid.shape[1]
    nt1 = nt2 // 2
    per_dev = images[1]
    sizes = (exc, np2, np1, nt2, images[0], per_dev)
    f32 = jnp.float32
    return pl.pallas_call(
        lambda *refs: coef_kernel(sizes, *refs),
        in_specs=[SMEM] * 5 + [VMEM] * 5,
        out_specs=[VMEM] * 7,
        out_shape=[
            jax.ShapeDtypeStruct((np2, 8 * per_dev, exc, LANES), f32),
            jax.ShapeDtypeStruct((np2 * 3, exc, LANES), f32),
            jax.ShapeDtypeStruct((np1 * 3, exc, LANES), f32),
            jax.ShapeDtypeStruct((2 * nt2, 2 * LANES), jnp.bfloat16),
            jax.ShapeDtypeStruct((4 * nt1, 2 * LANES), jnp.bfloat16),
            jax.ShapeDtypeStruct((4 * np1, LANES), f32),
            jax.ShapeDtypeStruct((4 * np1, LANES), f32),
        ],
        scratch_shapes=[
            pltpu.VMEM((2, np2, LANES), f32),
            pltpu.VMEM((8 * per_dev, np2, LANES), f32),
            pltpu.VMEM((2, images[0], LANES), f32),
            pltpu.VMEM((LANES, 2 * nt2), f32),
        ],
        compiler_params=pltpu.CompilerParams(vmem_limit_bytes=(8 << 20) + np2 * (96 << 10)),
        name="coefficients",
    )(where, inc, child, phi_top, phi_mid, img, tit, twt, tim, twm)


def split_dot(x, m_ref):
    high = x.astype(jnp.bfloat16)
    low = (x - high.astype(jnp.float32)).astype(jnp.bfloat16)
    wide = jnp.dot(high, m_ref[...], preferred_element_type=jnp.float32)
    rest = jnp.dot(low, m_ref[:, :LANES], preferred_element_type=jnp.float32)
    return wide[:, :LANES] + (wide[:, LANES:] + rest)


def phi_pass(count, contribution, emit):
    first = contribution(count - 1)
    second = contribution(0)
    carry = [x + y for x, y in zip(first[2], second[1])], list(second[2])

    def step(q, carry):
        here, after = carry
        new = contribution((q + 1) % count if isinstance(q, int) else lax.rem(q + 1, count))
        emit(q, [x + y for x, y in zip(here, new[0])])
        return [x + y for x, y in zip(after, new[1])], list(new[2])

    if count <= 16:
        for q in range(count):
            carry = step(q, carry)
    else:
        lax.fori_loop(0, count, step, carry)


def main_kernel(
    sizes,
    r_ref,
    w_ref,
    pw2_ref,
    pw1_ref,
    m2_ref,
    m1_ref,
    tc_ref,
    ts_ref,
    o_ref,
    x_ref,
    g_ref,
    h_ref,
    y_ref,
    z_ref,
):
    exc, np2, np1, nt2, phi_local, per_dev = sizes
    np0 = np1 // 2
    mid_local = phi_local // 2
    base = phi_local * per_dev * 2
    mids = 4 * per_dev

    for box in range(per_dev):

        def top(m, box=box):
            out = [[None] * 8 for _ in range(3)]
            for parity in range(2):
                p = 2 * m + parity
                tile = ((p % phi_local) * per_dev + box) * 2
                ar = r_ref[p // phi_local, tile]
                ai = r_ref[p // phi_local, tile + 1]
                weights = [pw2_ref[3 * p + s] for s in range(3)]
                for slot in range(4):
                    wr = w_ref[p, box * 8 + slot * 2]
                    wi = w_ref[p, box * 8 + slot * 2 + 1]
                    for c, value in enumerate(cmul(ar, ai, wr, wi)):
                        for s in range(3):
                            term = weights[s] * value
                            k = slot * 2 + c
                            out[s][k] = term if out[s][k] is None else out[s][k] + term
            return out

        def keep(q, values):
            for slot in range(4):
                for c in range(2):
                    x_ref[
                        pl.ds((q * 4 + slot) * exc, exc), c * LANES : (c + 1) * LANES
                    ] = values[slot * 2 + c]

        phi_pass(np1, top, keep)
        rows = x_ref.shape[0]
        block = min(rows, 512)

        def theta(part, box=box):
            done = split_dot(x_ref[pl.ds(part * block, block), :], m2_ref)
            per_block = block // (4 * exc)
            for n in range(per_block):
                q = part * per_block + n
                for slot in range(4):
                    row = (n * 4 + slot) * exc
                    mid = box * 4 + slot
                    value = (
                        done[row : row + exc]
                        + r_ref[q // mid_local, base + (q % mid_local) * mids + mid]
                    )
                    g_ref[q, mid] = value
                    h_ref[q, mid] = pltpu.roll(value, LANES // 2, 1)

        loop(rows // block, theta)

    o_rows = o_ref.reshape(exc * 4 * mids, o_ref.shape[2])

    for octant in range(4):
        for box in range(per_dev):

            def middle(m, octant=octant, box=box):
                out = [[None] * 4 for _ in range(3)]
                for parity in range(2):
                    q = 2 * m + parity
                    cosine = tc_ref[pl.ds(octant * np1 + q, 1), :]
                    sine = ts_ref[pl.ds(octant * np1 + q, 1), :]
                    weights = [pw1_ref[3 * q + s] for s in range(3)]
                    for slot in range(4):
                        value = (
                            g_ref[q, box * 4 + slot] * cosine + h_ref[q, box * 4 + slot] * sine
                        )
                        for s in range(3):
                            term = weights[s] * value
                            out[s][slot] = term if out[s][slot] is None else out[s][slot] + term
                return out

            def keep_low(q, values, octant=octant, box=box):
                for slot in range(4):
                    k = (box * 4 + slot) * 4 + octant
                    y_ref[q // 2, pl.ds(k * exc, exc), pl.ds((q % 2) * LANES, LANES)] = values[
                        slot
                    ]

            phi_pass(np0, middle, keep_low)

    def finish(pair):
        done = split_dot(y_ref[pair], m1_ref)
        start = pair * LANES
        lanes = pl.ds(start if isinstance(pair, int) else pl.multiple_of(start, LANES), LANES)
        for k in range(4 * mids):
            z_ref[pl.ds(k, exc, stride=4 * mids), :] = done[k * exc : (k + 1) * exc]
        o_rows[:, lanes] = z_ref[...]

    loop(np0 // 2, finish)


def main(received, coefs, exc, np2, np1, nt2, phi_local, per_dev):
    mids = 4 * per_dev
    np0 = np1 // 2
    f32 = jnp.float32
    sizes = (exc, np2, np1, nt2, phi_local, per_dev)
    return pl.pallas_call(
        lambda *refs: main_kernel(sizes, *refs),
        in_specs=[VMEM] * 8,
        out_specs=VMEM,
        out_shape=jax.ShapeDtypeStruct((exc, 4 * mids, np0 * (nt2 // 2)), f32),
        scratch_shapes=[
            pltpu.VMEM((np1 * 4 * exc, 2 * LANES), f32),
            pltpu.VMEM((np1, mids, exc, LANES), f32),
            pltpu.VMEM((np1, mids, exc, LANES), f32),
            pltpu.VMEM((np0 // 2, 4 * mids * exc, 2 * LANES), f32),
            pltpu.VMEM((4 * mids * exc, LANES), f32),
        ],
        compiler_params=pltpu.CompilerParams(vmem_limit_bytes=(8 << 20) + np2 * (144 << 10)),
        name="levels",
    )(received, *coefs)


def local(
    top_adj,
    level1_adj,
    image_offsets,
    image_weights,
    incidence,
    child_list,
    theta_index_top,
    theta_weight_top,
    phi_weight_top,
    theta_index_mid,
    theta_weight_mid,
    phi_weight_mid,
):
    dev_count = lax.axis_size("dev")
    rhs_count = lax.axis_size("rhs")
    exc, phi_local, top_boxes, top_width = top_adj.shape
    per_dev = top_boxes // dev_count
    nt2 = top_width // 2
    np2 = phi_local * dev_count
    np1 = np2 // 2
    images = image_offsets.shape[0] * rhs_count

    packed = pack(top_adj, level1_adj, dev_count)
    received = lax.all_to_all(packed, "dev", split_axis=0, concat_axis=0, tiled=True)

    own = jnp.concatenate(
        [
            image_offsets.T.astype(jnp.float32),
            image_weights[None] * float(images) ** (-0.5),
        ],
        axis=0,
    )
    parts = [own]
    for shift in range(1, rhs_count):
        parts.append(
            lax.ppermute(own, "rhs", [(i, (i + shift) % rhs_count) for i in range(rhs_count)])
        )
    img = jnp.concatenate(parts + [jnp.zeros((3, LANES - images), jnp.float32)], axis=1)
    where = jnp.stack([lax.axis_index("dev"), lax.axis_index("rhs")]).astype(jnp.int32)
    coefs = coefficients(
        where,
        incidence.T,
        child_list,
        phi_weight_top.T,
        phi_weight_mid.T,
        img,
        theta_index_top.T,
        theta_weight_top.T,
        theta_index_mid.T,
        theta_weight_mid.T,
        exc,
        nt2,
        (images, per_dev),
    )
    return main(received, coefs, exc, np2, np1, nt2, phi_local, per_dev)


def solution(mesh):
    placed = (
        P("rhs", "dev", None, None),
        P("rhs", "dev", None, None),
        P("rhs", None),
        P("rhs"),
        P(),
        P(),
        P(),
        P(),
        P(),
        P(),
        P(),
        P(),
    )
    return jax.shard_map(
        local, mesh=mesh, in_specs=placed, out_specs=P("rhs", "dev", None), check_vma=False
    )
```

```python
import math

import jax
import jax.numpy as jnp
from jax import lax
from jax.experimental import pallas as pl
from jax.experimental.pallas import tpu as pltpu
from jax.sharding import PartitionSpec as P

PHASE_TOP = 18.85
PHASE_MID = 9.42
LATTICE = 12.57
LANES = 128
HIGHEST = lax.Precision.HIGHEST
VMEM = pl.BlockSpec(memory_space=pltpu.VMEM)
SMEM = pl.BlockSpec(memory_space=pltpu.SMEM)


def sincos(x):
    n = jnp.floor(x * (2.0 / math.pi) + 0.5)
    r = x - n * 1.5703125
    r = r - n * 4.837512969970703125e-4
    r = r - n * 7.54978995489188216e-8
    z = r * r
    s = r + r * z * (-1.6666654611e-1 + z * (8.3321608736e-3 - z * 1.9515295891e-4))
    c = (1.0 - 0.5 * z) + z * z * (
        4.166664568298827e-2 + z * (-1.388731625493765e-3 + z * 2.443315711809948e-5)
    )
    quadrant = n.astype(jnp.int32)
    swap = (quadrant & 1) == 1
    sine = jnp.where(swap, c, s)
    cosine = jnp.where(swap, s, c)
    sine = jnp.where((quadrant & 2) == 2, -sine, sine)
    cosine = jnp.where(((quadrant + 1) & 2) == 2, -cosine, cosine)
    return sine, cosine


def directions(shape, theta_count, phi_count, row0=0):
    rows = lax.broadcasted_iota(jnp.int32, shape, 0).astype(jnp.float32) + row0
    cols = lax.broadcasted_iota(jnp.int32, shape, 1)
    theta = math.pi / theta_count * ((cols % theta_count).astype(jnp.float32) + 0.5)
    sin_theta, cos_theta = sincos(theta)
    sin_phi, cos_phi = sincos(2.0 * math.pi / phi_count * rows)
    return cos_phi * sin_theta, sin_phi * sin_theta, cos_theta


def cmul(ar, ai, br, bi):
    return ar * br - ai * bi, ar * bi + ai * br


def loop(count, body):
    if count <= 16:
        for step in range(count):
            body(step)
    else:
        lax.fori_loop(0, count, lambda step, carry: (body(step), carry)[1], 0)


def pack_kernel(per_dest, a_hbm, l_hbm, o_hbm, re_ref, im_ref, mid_ref, top_out, mid_out, sems):
    exc, phi_local, boxes, _ = re_ref.shape
    mid_phi, mids = mid_ref.shape[1:3]
    arrive = [
        pltpu.make_async_copy(a_hbm.at[:, :, :, pl.ds(0, LANES)], re_ref, sems.at[0]),
        pltpu.make_async_copy(a_hbm.at[:, :, :, pl.ds(LANES, LANES)], im_ref, sems.at[1]),
        pltpu.make_async_copy(l_hbm, mid_ref, sems.at[2]),
    ]
    for copy in arrive:
        copy.start()
    group = 8
    leave = []

    def scatter(source, target, dests):
        count, width, _ = source.shape
        rows = target.reshape(width * count, LANES)

        def one(g):
            for e in range(count):
                start = g * group * count + e
                rows[pl.ds(start, group, stride=count), :] = source[e, pl.ds(g * group, group), :]

        loop(width // group, one)
        split = target.reshape(width // len(dests), len(dests), count, LANES)
        for n, tile in enumerate(dests):
            copy = pltpu.make_async_copy(
                split.at[:, n], o_hbm.at[:, tile], sems.at[3 + len(leave)]
            )
            copy.start()
            leave.append(copy)

    for part, ref in enumerate((re_ref, im_ref)):
        arrive[part].wait()
        for phi in range(phi_local):
            k = phi * 2 + part
            scatter(
                ref.at[:, phi],
                top_out.at[k],
                [box * phi_local * 2 + k for box in range(per_dest)],
            )
    arrive[2].wait()
    first = per_dest * phi_local * 2
    for phi in range(mid_phi):
        scatter(
            mid_ref.at[:, phi],
            mid_out.at[phi],
            [first + mid * mid_phi + phi for mid in range(4 * per_dest)],
        )
    for copy in leave:
        copy.wait()


def pack(top_adj, level1_adj, dev_count):
    exc, phi_local, boxes, _ = top_adj.shape
    mid_phi, mids = level1_adj.shape[1:3]
    per_dest = boxes // dev_count
    tiles = (phi_local * 2 + mid_phi * 4) * per_dest
    f32 = jnp.float32
    hbm = pl.BlockSpec(memory_space=pltpu.HBM)
    return pl.pallas_call(
        lambda *refs: pack_kernel(per_dest, *refs),
        in_specs=[hbm] * 2,
        out_specs=hbm,
        out_shape=jax.ShapeDtypeStruct((dev_count, tiles, exc, LANES), f32),
        scratch_shapes=[
            pltpu.VMEM((exc, phi_local, boxes, LANES), f32),
            pltpu.VMEM((exc, phi_local, boxes, LANES), f32),
            pltpu.VMEM((exc, mid_phi, mids, LANES), f32),
            pltpu.VMEM((phi_local * 2, boxes, exc, LANES), f32),
            pltpu.VMEM((mid_phi, mids, exc, LANES), f32),
            pltpu.SemaphoreType.DMA((3 + tiles,)),
        ],
        compiler_params=pltpu.CompilerParams(vmem_limit_bytes=67043328),
        name="pack",
    )(top_adj, level1_adj)


def theta_block(index_ref, weight_ref, columns):
    samples = index_ref.shape[1]
    rows = lax.broadcasted_iota(jnp.int32, (columns, samples), 0)
    total = jnp.zeros((columns, samples), jnp.float32)
    for s in range(3):
        hit = rows == index_ref[s : s + 1, :]
        total = total + jnp.where(hit, weight_ref[s : s + 1, :], 0.0)
    return total


def coef_kernel(
    sizes,
    where_ref,
    inc_ref,
    child_ref,
    phi_top_ref,
    phi_mid_ref,
    img_ref,
    index_top_ref,
    weight_top_ref,
    index_mid_ref,
    weight_mid_ref,
    w_ref,
    pw2_ref,
    pw1_ref,
    m2_ref,
    m1_ref,
    tc_ref,
    ts_ref,
    dir_ref,
    ph_ref,
    ob_ref,
    fm_ref,
):
    exc, np2, np1, nt2, images, per_dev = sizes
    nt1, nt0 = nt2 // 2, nt2 // 4
    half = np2 // 2
    first_box = where_ref[0] * per_dev
    first_exc = where_ref[1] * exc

    def splat_top(p):
        for s in range(3):
            pw2_ref[p * 3 + s] = jnp.full((exc, LANES), phi_top_ref[s, p], jnp.float32)

    def splat_mid(p):
        for s in range(3):
            pw1_ref[p * 3 + s] = jnp.full((exc, LANES), phi_mid_ref[s, p], jnp.float32)

    loop(np2, splat_top)
    loop(np1, splat_mid)

    theta_top = theta_block(index_top_ref, weight_top_ref, nt1)
    theta_mid = theta_block(index_mid_ref, weight_mid_ref, nt0)
    for parts, block, m_ref in ((2, theta_top, m2_ref), (4, theta_mid, m1_ref)):
        high, width = block.shape
        fm_ref[...] = jnp.zeros(fm_ref.shape, jnp.float32)
        for part in range(parts):
            fm_ref[part * high : (part + 1) * high, part * width : (part + 1) * width] = block
        full = jnp.transpose(fm_ref[...])
        coarse = full.astype(jnp.bfloat16)
        m_ref[:, :LANES] = coarse
        m_ref[:, LANES:] = (full - coarse.astype(jnp.float32)).astype(jnp.bfloat16)

    mx, my, mz = directions((np1, LANES), nt1, np1)
    sxs, sxc = sincos(PHASE_MID * mx)
    sys_, syc = sincos(PHASE_MID * my)
    szs, szc = sincos(PHASE_MID * mz)
    lane = lax.broadcasted_iota(jnp.int32, (np1, LANES), 1)
    sign = jnp.where(lane < nt1, -1.0, 1.0)
    for octant in range(4):
        fx = 2.0 * (octant % 2) - 1.0
        fy = 2.0 * (octant // 2) - 1.0
        re, im = cmul(sxc, fx * sxs, syc, fy * sys_)
        re, im = cmul(re, im, szc, -szs)
        tc_ref[octant * np1 : (octant + 1) * np1, :] = re
        ts_ref[octant * np1 : (octant + 1) * np1, :] = im * sign

    ux, uy, uz = directions((np2, LANES), nt2, np2)
    dir_ref[0] = ux
    dir_ref[1] = uy
    axs, axc = sincos(PHASE_TOP * ux)
    ays, ayc = sincos(PHASE_TOP * uy)
    azs, azc = sincos(PHASE_TOP * uz)
    for box in range(per_dev):
        for slot in range(4):
            fx = jnp.float32(0.0)
            fy = jnp.float32(0.0)
            for octant in range(4):
                hit = child_ref[first_box + box, octant] == 4 * (first_box + box) + slot
                fx = fx + jnp.where(hit, jnp.float32(2.0 * (octant % 2) - 1.0), jnp.float32(0.0))
                fy = fy + jnp.where(hit, jnp.float32(2.0 * (octant // 2) - 1.0), jnp.float32(0.0))
            re, im = cmul(axc, fx * axs, ayc, fy * ays)
            re, im = cmul(re, im, azc, -azs)
            ph_ref[box * 8 + slot * 2] = re
            ph_ref[box * 8 + slot * 2 + 1] = im

    image = img_ref[...]
    ox, oy, wt = image[0:1, :], image[1:2, :], image[2:3, :]
    excs = lax.broadcasted_iota(jnp.int32, (exc, LANES), 0)
    kx = jnp.zeros((exc, LANES), jnp.float32)
    ky = jnp.zeros((exc, LANES), jnp.float32)
    for e in range(exc):
        kx = jnp.where(excs == e, inc_ref[0, first_exc + e], kx)
        ky = jnp.where(excs == e, inc_ref[1, first_exc + e], ky)
    fs, fc = sincos(LATTICE * (ox * kx + oy * ky))
    wc = (wt * fc)[:, :images]
    ws = (wt * fs)[:, :images]
    left_c = jnp.concatenate([wc, -ws, wc, -ws], axis=0)
    left_s = jnp.concatenate([ws, wc, -ws, -wc], axis=0)
    ob_ref[0] = jnp.transpose(jnp.broadcast_to(LATTICE * ox, (LANES, LANES)))[:images]
    ob_ref[1] = jnp.transpose(jnp.broadcast_to(LATTICE * oy, (LANES, LANES)))[:images]

    def lattice(p):
        ux_row = dir_ref[0, pl.ds(p, 1), :]
        uy_row = dir_ref[1, pl.ds(p, 1), :]
        sb, cb = sincos(ob_ref[0] * ux_row + ob_ref[1] * uy_row)
        total = jnp.dot(
            left_c, cb, precision=HIGHEST, preferred_element_type=jnp.float32
        ) + jnp.dot(left_s, sb, precision=HIGHEST, preferred_element_type=jnp.float32)
        for mirror in range(2):
            sr = total[(2 * mirror) * exc : (2 * mirror + 1) * exc]
            si = total[(2 * mirror + 1) * exc : (2 * mirror + 2) * exc]
            q = p + mirror * half
            for tile in range(4 * per_dev):
                pr = ph_ref[2 * tile, pl.ds(q, 1), :]
                pi = ph_ref[2 * tile + 1, pl.ds(q, 1), :]
                re, im = cmul(pr, pi, sr, -si)
                w_ref[q, 2 * tile] = re
                w_ref[q, 2 * tile + 1] = im

    loop(half, lattice)


def coefficients(where, inc, child, phi_top, phi_mid, img, tit, twt, tim, twm, exc, nt2, images):
    np2, np1 = phi_top.shape[1], phi_mid.shape[1]
    nt1 = nt2 // 2
    per_dev = images[1]
    sizes = (exc, np2, np1, nt2, images[0], per_dev)
    f32 = jnp.float32
    return pl.pallas_call(
        lambda *refs: coef_kernel(sizes, *refs),
        in_specs=[SMEM] * 5 + [VMEM] * 5,
        out_specs=[VMEM] * 7,
        out_shape=[
            jax.ShapeDtypeStruct((np2, 8 * per_dev, exc, LANES), f32),
            jax.ShapeDtypeStruct((np2 * 3, exc, LANES), f32),
            jax.ShapeDtypeStruct((np1 * 3, exc, LANES), f32),
            jax.ShapeDtypeStruct((2 * nt2, 2 * LANES), jnp.bfloat16),
            jax.ShapeDtypeStruct((4 * nt1, 2 * LANES), jnp.bfloat16),
            jax.ShapeDtypeStruct((4 * np1, LANES), f32),
            jax.ShapeDtypeStruct((4 * np1, LANES), f32),
        ],
        scratch_shapes=[
            pltpu.VMEM((2, np2, LANES), f32),
            pltpu.VMEM((8 * per_dev, np2, LANES), f32),
            pltpu.VMEM((2, images[0], LANES), f32),
            pltpu.VMEM((LANES, 2 * nt2), f32),
        ],
        compiler_params=pltpu.CompilerParams(vmem_limit_bytes=(8 << 20) + np2 * (96 << 10)),
        name="coefficients",
    )(where, inc, child, phi_top, phi_mid, img, tit, twt, tim, twm)


def split_dot(x, m_ref):
    high = x.astype(jnp.bfloat16)
    low = (x - high.astype(jnp.float32)).astype(jnp.bfloat16)
    wide = jnp.dot(high, m_ref[...], preferred_element_type=jnp.float32)
    rest = jnp.dot(low, m_ref[:, :LANES], preferred_element_type=jnp.float32)
    return wide[:, :LANES] + (wide[:, LANES:] + rest)


def phi_pass(count, contribution, emit, origin=0):
    if count <= 16:
        first = contribution(origin % count)
        here, after = first[1], first[2]
        held = None
        for m in range(1, count):
            new = contribution((m + origin) % count)
            ready = [x + y for x, y in zip(here, new[0])]
            if m == 1:
                held = ready
            else:
                emit((m - 1 + origin) % count, ready)
            here, after = [x + y for x, y in zip(after, new[1])], new[2]
        emit((count - 1 + origin) % count, [x + y for x, y in zip(here, first[0])])
        emit(origin % count, [x + y for x, y in zip(held, after)])
        return

    first = contribution(count - 1)
    second = contribution(0)

    def step(q, carry):
        here, after = carry
        new = contribution(lax.rem(q + 1, count))
        emit(q, [x + y for x, y in zip(here, new[0])])
        return [x + y for x, y in zip(after, new[1])], list(new[2])

    lax.fori_loop(
        0, count, step, ([x + y for x, y in zip(first[2], second[1])], list(second[2]))
    )


def main_kernel(
    sizes,
    r_ref,
    w_ref,
    pw2_ref,
    pw1_ref,
    m2_ref,
    m1_ref,
    tc_ref,
    ts_ref,
    o_ref,
    x_ref,
    g_ref,
    h_ref,
    y_ref,
    z_ref,
    sems,
):
    exc, np2, np1, nt2, phi_local, per_dev = sizes
    np0 = np1 // 2
    mid_local = phi_local // 2
    base = phi_local * per_dev * 2
    mids = 4 * per_dev

    for box in range(per_dev):

        def top(m, box=box):
            out = [[None] * 8 for _ in range(3)]
            for parity in range(2):
                p = 2 * m + parity
                tile = (box * phi_local + p % phi_local) * 2
                ar = r_ref[p // phi_local, tile]
                ai = r_ref[p // phi_local, tile + 1]
                weights = [pw2_ref[3 * p + s] for s in range(3)]
                for slot in range(4):
                    wr = w_ref[p, box * 8 + slot * 2]
                    wi = w_ref[p, box * 8 + slot * 2 + 1]
                    for c, value in enumerate(cmul(ar, ai, wr, wi)):
                        for s in range(3):
                            term = weights[s] * value
                            k = slot * 2 + c
                            out[s][k] = term if out[s][k] is None else out[s][k] + term
            return out

        chunk = min(np1, 4)

        def theta(part, box=box):
            done = split_dot(x_ref[pl.ds(part * chunk * 4 * exc, chunk * 4 * exc), :], m2_ref)
            for n in range(chunk):
                q = (part * chunk + n + 1) % np1
                for slot in range(4):
                    row = (n * 4 + slot) * exc
                    mid = box * 4 + slot
                    value = (
                        done[row : row + exc]
                        + r_ref[q // mid_local, base + mid * mid_local + q % mid_local]
                    )
                    g_ref[q, mid] = value
                    h_ref[q, mid] = pltpu.roll(value, LANES // 2, 1)

        static = np1 <= 16

        def keep(q, values):
            place = (q + np1 - 1) % np1
            for slot in range(4):
                for c in range(2):
                    x_ref[
                        pl.ds((place * 4 + slot) * exc, exc), c * LANES : (c + 1) * LANES
                    ] = values[slot * 2 + c]
            if static and place % chunk == chunk - 1:
                theta(place // chunk)

        phi_pass(np1, top, keep)
        if not static:
            loop(np1 // chunk, theta)

    o_rows = o_ref.reshape(exc * 4 * mids, o_ref.shape[2])

    pairs = np0 // 2

    for octant in range(4):
        for box in range(per_dev):

            def middle(m, octant=octant, box=box):
                out = [[None] * 4 for _ in range(3)]
                for parity in range(2):
                    q = 2 * m + parity
                    cosine = tc_ref[pl.ds(octant * np1 + q, 1), :]
                    sine = ts_ref[pl.ds(octant * np1 + q, 1), :]
                    weights = [pw1_ref[3 * q + s] for s in range(3)]
                    for slot in range(4):
                        value = (
                            g_ref[q, box * 4 + slot] * cosine + h_ref[q, box * 4 + slot] * sine
                        )
                        for s in range(3):
                            term = weights[s] * value
                            out[s][slot] = term if out[s][slot] is None else out[s][slot] + term
                return out

            buffer = y_ref.at[octant % 2]

            def keep_low(q, values, buffer=buffer):
                for slot in range(4):
                    buffer[q // 2, pl.ds(slot * exc, exc), pl.ds((q % 2) * LANES, LANES)] = (
                        values[slot]
                    )

            phi_pass(np0, middle, keep_low, 1)

            def finish(part, octant=octant, box=box, buffer=buffer):
                step = min(pairs, 4)
                tile = buffer[pl.ds(part * step, step)].reshape(step * 4 * exc, 2 * LANES)
                done = split_dot(tile, m1_ref)
                for n in range(step):
                    for slot in range(4):
                        k = (box * 4 + slot) * 4 + octant
                        row = (n * 4 + slot) * exc
                        z_ref[part * step + n, pl.ds(k, exc, stride=4 * mids), :] = done[
                            row : row + exc
                        ]

            loop(pairs // min(pairs, 4), finish)

    def leave(pair):
        start = pair * LANES
        lanes = pl.ds(start if isinstance(pair, int) else pl.multiple_of(start, LANES), LANES)
        return pltpu.make_async_copy(z_ref.at[pair], o_rows.at[:, lanes], sems.at[pair])

    loop(pairs, lambda pair: leave(pair).start())
    loop(pairs, lambda pair: leave(pair).wait())


def main(received, coefs, exc, np2, np1, nt2, phi_local, per_dev):
    mids = 4 * per_dev
    np0 = np1 // 2
    f32 = jnp.float32
    sizes = (exc, np2, np1, nt2, phi_local, per_dev)
    return pl.pallas_call(
        lambda *refs: main_kernel(sizes, *refs),
        in_specs=[VMEM] * 8,
        out_specs=pl.BlockSpec(memory_space=pltpu.HBM),
        out_shape=jax.ShapeDtypeStruct((exc, 4 * mids, np0 * (nt2 // 2)), f32),
        scratch_shapes=[
            pltpu.VMEM((np1 * 4 * exc, 2 * LANES), f32),
            pltpu.VMEM((np1, mids, exc, LANES), f32),
            pltpu.VMEM((np1, mids, exc, LANES), f32),
            pltpu.VMEM((2, np0 // 2, 4 * exc, 2 * LANES), f32),
            pltpu.VMEM((np0 // 2, 4 * mids * exc, LANES), f32),
            pltpu.SemaphoreType.DMA((np0 // 2,)),
        ],
        compiler_params=pltpu.CompilerParams(vmem_limit_bytes=(8 << 20) + np2 * (144 << 10)),
        name="levels",
    )(received, *coefs)


def local(
    top_adj,
    level1_adj,
    image_offsets,
    image_weights,
    incidence,
    child_list,
    theta_index_top,
    theta_weight_top,
    phi_weight_top,
    theta_index_mid,
    theta_weight_mid,
    phi_weight_mid,
):
    dev_count = lax.axis_size("dev")
    rhs_count = lax.axis_size("rhs")
    exc, phi_local, top_boxes, top_width = top_adj.shape
    per_dev = top_boxes // dev_count
    nt2 = top_width // 2
    np2 = phi_local * dev_count
    np1 = np2 // 2
    images = image_offsets.shape[0] * rhs_count

    packed = pack(top_adj, level1_adj, dev_count)
    received = lax.all_to_all(packed, "dev", split_axis=0, concat_axis=0, tiled=True)

    own = jnp.concatenate(
        [
            image_offsets.T.astype(jnp.float32),
            image_weights[None] * float(images) ** (-0.5),
        ],
        axis=0,
    )
    parts = [own]
    for shift in range(1, rhs_count):
        parts.append(
            lax.ppermute(own, "rhs", [(i, (i + shift) % rhs_count) for i in range(rhs_count)])
        )
    img = jnp.concatenate(parts + [jnp.zeros((3, LANES - images), jnp.float32)], axis=1)
    where = jnp.stack([lax.axis_index("dev"), lax.axis_index("rhs")]).astype(jnp.int32)
    coefs = coefficients(
        where,
        incidence.T,
        child_list,
        phi_weight_top.T,
        phi_weight_mid.T,
        img,
        theta_index_top.T,
        theta_weight_top.T,
        theta_index_mid.T,
        theta_weight_mid.T,
        exc,
        nt2,
        (images, per_dev),
    )
    return main(received, coefs, exc, np2, np1, nt2, phi_local, per_dev)


def solution(mesh):
    placed = (
        P("rhs", "dev", None, None),
        P("rhs", "dev", None, None),
        P("rhs", None),
        P("rhs"),
        P(),
        P(),
        P(),
        P(),
        P(),
        P(),
        P(),
        P(),
    )
    return jax.shard_map(
        local, mesh=mesh, in_specs=placed, out_specs=P("rhs", "dev", None), check_vma=False
    )
```

```python
import math

import jax
import jax.numpy as jnp
from jax import lax
from jax.experimental import pallas as pl
from jax.experimental.pallas import tpu as pltpu
from jax.sharding import PartitionSpec as P


PHASE_TOP = 18.85
PHASE_MID = 9.42
LATTICE = 12.57
LANES = 128
VMEM = pl.BlockSpec(memory_space=pltpu.VMEM)
SMEM = pl.BlockSpec(memory_space=pltpu.SMEM)


SINE = (3.141592502593994, -5.1677069664001465, 2.5500314235687256, -0.5980451703071594, 0.0772201269865036)
COSINE = (1.0, -4.934802055358887, 4.058709144592285, -1.3352121114730835, 0.23493756353855133, -0.024396715685725212)


def horner(z, factors):
    total = factors[-1]
    for factor in factors[-2::-1]:
        total = total * z + factor
    return total


def sincos(x):
    n = jnp.floor(x + 0.5)
    f = x - n
    z = f * f
    sign = jnp.where((n.astype(jnp.int32) & 1) == 1, -1.0, 1.0)
    return sign * f * horner(z, SINE), sign * horner(z, COSINE)


def directions(shape, theta_count, phi_count):
    rows = lax.broadcasted_iota(jnp.int32, shape, 0).astype(jnp.float32)
    cols = lax.broadcasted_iota(jnp.int32, shape, 1)
    theta = ((cols % theta_count).astype(jnp.float32) + 0.5) / theta_count
    sin_theta, cos_theta = sincos(theta)
    sin_phi, cos_phi = sincos(2.0 / phi_count * rows)
    return cos_phi * sin_theta, sin_phi * sin_theta, cos_theta


def cmul(ar, ai, br, bi):
    return ar * br - ai * bi, ar * bi + ai * br


def loop(count, body):
    if count <= 16:
        for step in range(count):
            body(step)
    else:
        lax.fori_loop(0, count, lambda step, carry: (body(step), carry)[1], 0)


def factors(dev_count):
    inner = 1 << ((dev_count.bit_length() - 1) // 2)
    return dev_count // inner, inner


def pack_kernel(per_dest, outer, inner, a_hbm, l_hbm, mid_hbm, *refs):
    top_hbm = refs[:outer]
    re_ref, im_ref, mid_ref, top_out, mid_out, sems = refs[outer:]
    exc, phi_local, boxes, _ = re_ref.shape
    mid_phi, _ = mid_ref.shape[1:3]
    plane = lax.axis_index("dev") // inner
    arrive = [
        pltpu.make_async_copy(a_hbm.at[:, :, :, pl.ds(0, LANES)], re_ref, sems.at[0]),
        pltpu.make_async_copy(a_hbm.at[:, :, :, pl.ds(LANES, LANES)], im_ref, sems.at[1]),
        pltpu.make_async_copy(l_hbm, mid_ref, sems.at[2]),
    ]
    for copy in arrive:
        copy.start()
    group = 8
    leave = []

    def scatter(source, target):
        count, width, _ = source.shape
        rows = target.reshape(width * count, LANES)

        def one(g):
            for e in range(count):
                start = g * group * count + e
                rows[pl.ds(start, group, stride=count), :] = source[e, pl.ds(g * group, group), :]

        loop(width // group, one)

    def send(source, target):
        copy = pltpu.make_async_copy(source, target, sems.at[3 + len(leave)])
        copy.start()
        leave.append(copy)

    for part, ref in enumerate((re_ref, im_ref)):
        arrive[part].wait()
        for phi in range(phi_local):
            k = phi * 2 + part
            scatter(ref.at[:, phi], top_out.at[k])
            split = top_out.at[k].reshape(boxes // per_dest, per_dest, exc, LANES)
            for other in range(outer):
                for box in range(per_dest):
                    send(
                        split.at[pl.ds((plane ^ other) * inner, inner), box],
                        top_hbm[other].at[:, box * phi_local * 2 + k],
                    )
    arrive[2].wait()
    for phi in range(mid_phi):
        scatter(mid_ref.at[:, phi], mid_out.at[phi])
        split = mid_out.at[phi].reshape(boxes // per_dest, 4 * per_dest, exc, LANES)
        for mid in range(4 * per_dest):
            send(split.at[:, mid], mid_hbm.at[:, mid * mid_phi + phi])
    for copy in leave:
        copy.wait()


def pack(top_adj, level1_adj, dev_count):
    exc, phi_local, boxes, _ = top_adj.shape
    mid_phi, mids = level1_adj.shape[1:3]
    per_dest = boxes // dev_count
    outer, inner = factors(dev_count)
    tops = phi_local * 2 * per_dest
    f32 = jnp.float32
    hbm = pl.BlockSpec(memory_space=pltpu.HBM)
    return pl.pallas_call(
        lambda *refs: pack_kernel(per_dest, outer, inner, *refs),
        in_specs=[hbm] * 2,
        out_specs=[hbm] * (1 + outer),
        out_shape=[jax.ShapeDtypeStruct((dev_count, 4 * per_dest * mid_phi, exc, LANES), f32)]
        + [jax.ShapeDtypeStruct((inner, tops, exc, LANES), f32)] * outer,
        scratch_shapes=[
            pltpu.VMEM((exc, phi_local, boxes, LANES), f32),
            pltpu.VMEM((exc, phi_local, boxes, LANES), f32),
            pltpu.VMEM((exc, mid_phi, mids, LANES), f32),
            pltpu.VMEM((phi_local * 2, boxes, exc, LANES), f32),
            pltpu.VMEM((mid_phi, mids, exc, LANES), f32),
            pltpu.SemaphoreType.DMA((3 + outer * tops + 4 * per_dest * mid_phi,)),
        ],
        compiler_params=pltpu.CompilerParams(vmem_limit_bytes=67043328),
        name="pack",
    )(top_adj, level1_adj)


def theta_block(index_ref, weight_ref, columns):
    samples = index_ref.shape[1]
    rows = lax.broadcasted_iota(jnp.int32, (columns, samples), 0)
    total = jnp.zeros((columns, samples), jnp.float32)
    for s in range(3):
        hit = rows == index_ref[s : s + 1, :]
        total = total + jnp.where(hit, weight_ref[s : s + 1, :], 0.0)
    return total


def table_kernel(
    sizes,
    where_ref,
    child_ref,
    phi_top_ref,
    phi_mid_ref,
    index_top_ref,
    weight_top_ref,
    index_mid_ref,
    weight_mid_ref,
    pw2_ref,
    pw1_ref,
    m2_ref,
    m1_ref,
    tc_ref,
    ts_ref,
    dir_ref,
    ph_ref,
    fm_ref,
):
    exc, np2, np1, nt2, per_dev = sizes
    nt1, nt0 = nt2 // 2, nt2 // 4
    first_box = where_ref[0] * per_dev

    def splat_top(p):
        for s in range(3):
            pw2_ref[p * 3 + s] = jnp.full((exc, LANES), phi_top_ref[s, p], jnp.float32)

    def splat_mid(p):
        for s in range(3):
            pw1_ref[p * 3 + s] = jnp.full((exc, LANES), phi_mid_ref[s, p], jnp.float32)

    loop(np2, splat_top)
    loop(np1, splat_mid)

    theta_top = theta_block(index_top_ref, weight_top_ref, nt1)
    theta_mid = theta_block(index_mid_ref, weight_mid_ref, nt0)
    for parts, block, m_ref in ((2, theta_top, m2_ref), (4, theta_mid, m1_ref)):
        high, width = block.shape
        fm_ref[...] = jnp.zeros(fm_ref.shape, jnp.float32)
        for part in range(parts):
            fm_ref[part * high : (part + 1) * high, part * width : (part + 1) * width] = block
        full = jnp.transpose(fm_ref[...])
        coarse = full.astype(jnp.bfloat16)
        m_ref[:, :LANES] = coarse
        m_ref[:, LANES:] = (full - coarse.astype(jnp.float32)).astype(jnp.bfloat16)

    mx, my, mz = directions((np1, LANES), nt1, np1)
    sxs, sxc = sincos(PHASE_MID / math.pi * mx)
    sys_, syc = sincos(PHASE_MID / math.pi * my)
    szs, szc = sincos(PHASE_MID / math.pi * mz)
    lane = lax.broadcasted_iota(jnp.int32, (np1, LANES), 1)
    sign = jnp.where(lane < nt1, -1.0, 1.0)
    for octant in range(4):
        fx = 2.0 * (octant % 2) - 1.0
        fy = 2.0 * (octant // 2) - 1.0
        re, im = cmul(sxc, fx * sxs, syc, fy * sys_)
        re, im = cmul(re, im, szc, -szs)
        tc_ref[octant * np1 : (octant + 1) * np1, :] = re
        ts_ref[octant * np1 : (octant + 1) * np1, :] = im * sign

    ux, uy, uz = directions((np2, LANES), nt2, np2)
    dir_ref[0] = ux
    dir_ref[1] = uy
    axs, axc = sincos(PHASE_TOP / math.pi * ux)
    ays, ayc = sincos(PHASE_TOP / math.pi * uy)
    azs, azc = sincos(PHASE_TOP / math.pi * uz)
    for box in range(per_dev):
        for slot in range(4):
            fx = jnp.float32(0.0)
            fy = jnp.float32(0.0)
            for octant in range(4):
                hit = child_ref[first_box + box, octant] == 4 * (first_box + box) + slot
                fx = fx + jnp.where(hit, jnp.float32(2.0 * (octant % 2) - 1.0), jnp.float32(0.0))
                fy = fy + jnp.where(hit, jnp.float32(2.0 * (octant // 2) - 1.0), jnp.float32(0.0))
            re, im = cmul(axc, fx * axs, ayc, fy * ays)
            re, im = cmul(re, im, azc, -azs)
            ph_ref[box * 8 + slot * 2] = re
            ph_ref[box * 8 + slot * 2 + 1] = im


def lattice_kernel(
    sizes, where_ref, inc_ref, img_ref, dir_ref, ph_ref, w_ref, ob_ref
):
    exc, np2, images, per_dev = sizes
    half = np2 // 2
    first_exc = where_ref[1] * exc

    image = img_ref[...]
    ox, oy, wt = image[0:1, :], image[1:2, :], image[2:3, :]
    excs = lax.broadcasted_iota(jnp.int32, (exc, LANES), 0)
    kx = jnp.zeros((exc, LANES), jnp.float32)
    ky = jnp.zeros((exc, LANES), jnp.float32)
    for e in range(exc):
        kx = jnp.where(excs == e, inc_ref[0, first_exc + e], kx)
        ky = jnp.where(excs == e, inc_ref[1, first_exc + e], ky)
    fs, fc = sincos(LATTICE / math.pi * (ox * kx + oy * ky))
    wc = (wt * fc)[:, :images]
    ws = (wt * fs)[:, :images]
    left = jnp.concatenate(
        [
            jnp.concatenate([wc, -ws, wc, -ws], axis=0),
            jnp.concatenate([ws, wc, -ws, -wc], axis=0),
        ],
        axis=1,
    )
    left_high = left.astype(jnp.bfloat16)
    left_low = (left - left_high.astype(jnp.float32)).astype(jnp.bfloat16)
    left_both = jnp.concatenate([left_high, left_low], axis=0)
    ob_ref[0] = jnp.transpose(jnp.broadcast_to(LATTICE / math.pi * ox, (LANES, LANES)))[:images]
    ob_ref[1] = jnp.transpose(jnp.broadcast_to(LATTICE / math.pi * oy, (LANES, LANES)))[:images]

    def sample(p):
        ux_row = dir_ref[0, pl.ds(p, 1), :]
        uy_row = dir_ref[1, pl.ds(p, 1), :]
        sb, cb = sincos(ob_ref[0] * ux_row + ob_ref[1] * uy_row)
        basis = jnp.concatenate([cb, sb], axis=0)
        high = basis.astype(jnp.bfloat16)
        low = (basis - high.astype(jnp.float32)).astype(jnp.bfloat16)
        both = jnp.dot(left_both, high, preferred_element_type=jnp.float32)
        rest = jnp.dot(left_high, low, preferred_element_type=jnp.float32)
        total = both[: 4 * exc] + (both[4 * exc :] + rest)
        for mirror in range(2):
            sr = total[(2 * mirror) * exc : (2 * mirror + 1) * exc]
            si = total[(2 * mirror + 1) * exc : (2 * mirror + 2) * exc]
            q = p + mirror * half
            for tile in range(4 * per_dev):
                pr = ph_ref[2 * tile, pl.ds(q, 1), :]
                pi = ph_ref[2 * tile + 1, pl.ds(q, 1), :]
                re, im = cmul(pr, pi, sr, -si)
                w_ref[q, 2 * tile] = re
                w_ref[q, 2 * tile + 1] = im

    loop(half, sample)


def tables(where, child, phi_top, phi_mid, tit, twt, tim, twm, exc, nt2, per_dev):
    np2, np1 = phi_top.shape[1], phi_mid.shape[1]
    sizes = (exc, np2, np1, nt2, per_dev)
    f32 = jnp.float32
    return pl.pallas_call(
        lambda *refs: table_kernel(sizes, *refs),
        in_specs=[SMEM] * 4 + [VMEM] * 4,
        out_specs=[VMEM] * 8,
        out_shape=[
            jax.ShapeDtypeStruct((np2 * 3, exc, LANES), f32),
            jax.ShapeDtypeStruct((np1 * 3, exc, LANES), f32),
            jax.ShapeDtypeStruct((2 * nt2, 2 * LANES), jnp.bfloat16),
            jax.ShapeDtypeStruct((2 * nt2, 2 * LANES), jnp.bfloat16),
            jax.ShapeDtypeStruct((4 * np1, LANES), f32),
            jax.ShapeDtypeStruct((4 * np1, LANES), f32),
            jax.ShapeDtypeStruct((2, np2, LANES), f32),
            jax.ShapeDtypeStruct((8 * per_dev, np2, LANES), f32),
        ],
        scratch_shapes=[pltpu.VMEM((LANES, 2 * nt2), f32)],
        compiler_params=pltpu.CompilerParams(vmem_limit_bytes=(8 << 20) + np2 * (64 << 10)),
        name="tables",
    )(where, child, phi_top, phi_mid, tit, twt, tim, twm)


def lattice(where, inc, img, places, phases, exc, images):
    np2 = places.shape[1]
    per_dev = phases.shape[0] // 8
    f32 = jnp.float32
    return pl.pallas_call(
        lambda *refs: lattice_kernel((exc, np2, images, per_dev), *refs),
        in_specs=[SMEM] * 2 + [VMEM] * 3,
        out_specs=VMEM,
        out_shape=jax.ShapeDtypeStruct((np2, 8 * per_dev, exc, LANES), f32),
        scratch_shapes=[pltpu.VMEM((2, images, LANES), f32)],
        compiler_params=pltpu.CompilerParams(vmem_limit_bytes=(8 << 20) + np2 * (64 << 10)),
        name="lattice",
    )(where, inc, img, places, phases)


def split_dot(x, m_ref):
    high = x.astype(jnp.bfloat16)
    low = (x - high.astype(jnp.float32)).astype(jnp.bfloat16)
    wide = jnp.dot(high, m_ref[...], preferred_element_type=jnp.float32)
    rest = jnp.dot(low, m_ref[:, :LANES], preferred_element_type=jnp.float32)
    return wide[:, :LANES] + (wide[:, LANES:] + rest)


def phi_pass(count, contribution, emit, origin=0):
    if count <= 16:
        first = contribution(origin % count)
        here, after = first[1], first[2]
        held = None
        for m in range(1, count):
            new = contribution((m + origin) % count)
            ready = [x + y for x, y in zip(here, new[0])]
            if m == 1:
                held = ready
            else:
                emit((m - 1 + origin) % count, ready)
            here, after = [x + y for x, y in zip(after, new[1])], new[2]
        emit((count - 1 + origin) % count, [x + y for x, y in zip(here, first[0])])
        emit(origin % count, [x + y for x, y in zip(held, after)])
        return

    first = contribution(count - 1)
    second = contribution(0)

    def step(q, carry):
        here, after = carry
        new = contribution(lax.rem(q + 1, count))
        emit(q, [x + y for x, y in zip(here, new[0])])
        return [x + y for x, y in zip(after, new[1])], list(new[2])

    lax.fori_loop(
        0, count, step, ([x + y for x, y in zip(first[2], second[1])], list(second[2]))
    )


def upper_kernel(sizes, *refs):
    exc, _, np1, _, phi_local, per_dev, outer, inner = sizes
    parts = refs[:inner]
    w_ref, pw2_ref, m2_ref, u_ref, r_ref, x_ref = refs[inner:]
    me = lax.axis_index("dev")
    for j in range(inner):

        def place(k, j=j):
            source = ((me // inner) ^ k) * inner + ((me % inner) ^ j)
            r_ref[source] = parts[j][k]

        loop(outer, place)

    for box in range(per_dev):

        def top(m, box=box):
            out = [[None] * 8 for _ in range(3)]
            for parity in range(2):
                p = 2 * m + parity
                tile = (box * phi_local + p % phi_local) * 2
                ar = r_ref[p // phi_local, tile]
                ai = r_ref[p // phi_local, tile + 1]
                weights = [pw2_ref[3 * p + s] for s in range(3)]
                for slot in range(4):
                    wr = w_ref[p, box * 8 + slot * 2]
                    wi = w_ref[p, box * 8 + slot * 2 + 1]
                    for c, value in enumerate(cmul(ar, ai, wr, wi)):
                        for s in range(3):
                            term = weights[s] * value
                            k = slot * 2 + c
                            out[s][k] = term if out[s][k] is None else out[s][k] + term
            return out

        chunk = min(np1, 4)

        def theta(part, box=box):
            done = split_dot(x_ref[pl.ds(part * chunk * 4 * exc, chunk * 4 * exc), :], m2_ref)
            for n in range(chunk):
                q = (part * chunk + n + 1) % np1
                for slot in range(4):
                    row = (n * 4 + slot) * exc
                    mid = box * 4 + slot
                    u_ref[q, mid] = done[row : row + exc]

        static = np1 <= 16

        def keep(q, values):
            place = (q + np1 - 1) % np1
            for slot in range(4):
                for c in range(2):
                    x_ref[
                        pl.ds((place * 4 + slot) * exc, exc), c * LANES : (c + 1) * LANES
                    ] = values[slot * 2 + c]
            if static and place % chunk == chunk - 1:
                theta(place // chunk)

        phi_pass(np1, top, keep)
        if not static:
            loop(np1 // chunk, theta)


def lower_kernel(
    sizes, l_ref, u_ref, pw1_ref, m1_ref, tc_ref, ts_ref, o_ref, g_ref, h_ref, y_ref, z_ref, sems
):
    exc, np1, phi_local, per_dev = sizes
    np0 = np1 // 2
    mid_local = phi_local // 2
    mids = 4 * per_dev

    def join(q):
        for mid in range(mids):
            value = u_ref[q, mid] + l_ref[q // mid_local, mid * mid_local + q % mid_local]
            g_ref[q, mid] = value
            h_ref[q, mid] = pltpu.roll(value, LANES // 2, 1)

    loop(np1, join)
    o_rows = o_ref.reshape(exc * 4 * mids, o_ref.shape[2])

    pairs = np0 // 2

    for octant in range(4):
        for box in range(per_dev):

            def middle(m, octant=octant, box=box):
                out = [[None] * 4 for _ in range(3)]
                for parity in range(2):
                    q = 2 * m + parity
                    cosine = tc_ref[pl.ds(octant * np1 + q, 1), :]
                    sine = ts_ref[pl.ds(octant * np1 + q, 1), :]
                    weights = [pw1_ref[3 * q + s] for s in range(3)]
                    for slot in range(4):
                        value = (
                            g_ref[q, box * 4 + slot] * cosine + h_ref[q, box * 4 + slot] * sine
                        )
                        for s in range(3):
                            term = weights[s] * value
                            out[s][slot] = term if out[s][slot] is None else out[s][slot] + term
                return out

            buffer = y_ref.at[octant % 2]

            def keep_low(q, values, buffer=buffer):
                for slot in range(4):
                    buffer[q // 2, pl.ds(slot * exc, exc), pl.ds((q % 2) * LANES, LANES)] = (
                        values[slot]
                    )

            phi_pass(np0, middle, keep_low, 1)

            def finish(part, octant=octant, box=box, buffer=buffer):
                step = min(pairs, 4)
                tile = buffer[pl.ds(part * step, step)].reshape(step * 4 * exc, 2 * LANES)
                done = split_dot(tile, m1_ref)
                for n in range(step):
                    for slot in range(4):
                        k = (box * 4 + slot) * 4 + octant
                        row = (n * 4 + slot) * exc
                        z_ref[part * step + n, pl.ds(k, exc, stride=4 * mids), :] = done[
                            row : row + exc
                        ]

            loop(pairs // min(pairs, 4), finish)

    def leave(pair):
        start = pair * LANES
        lanes = pl.ds(start if isinstance(pair, int) else pl.multiple_of(start, LANES), LANES)
        return pltpu.make_async_copy(z_ref.at[pair], o_rows.at[:, lanes], sems.at[pair])

    loop(pairs, lambda pair: leave(pair).start())
    loop(pairs, lambda pair: leave(pair).wait())


def upper(parts, coefs, exc, np2, np1, nt2, phi_local, per_dev, outer, inner):
    f32 = jnp.float32
    sizes = (exc, np2, np1, nt2, phi_local, per_dev, outer, inner)
    tops = phi_local * 2 * per_dev
    return pl.pallas_call(
        lambda *refs: upper_kernel(sizes, *refs),
        in_specs=[VMEM] * (inner + 3),
        out_specs=VMEM,
        out_shape=jax.ShapeDtypeStruct((np1, 4 * per_dev, exc, LANES), f32),
        scratch_shapes=[
            pltpu.VMEM((outer * inner, tops, exc, LANES), f32),
            pltpu.VMEM((np1 * 4 * exc, 2 * LANES), f32),
        ],
        compiler_params=pltpu.CompilerParams(vmem_limit_bytes=(8 << 20) + np2 * (112 << 10)),
        name="upper",
    )(*parts, *coefs)


def lower(received, above, coefs, exc, np1, nt2, phi_local, per_dev):
    mids = 4 * per_dev
    np0 = np1 // 2
    f32 = jnp.float32
    sizes = (exc, np1, phi_local, per_dev)
    return pl.pallas_call(
        lambda *refs: lower_kernel(sizes, *refs),
        in_specs=[VMEM] * 6,
        out_specs=pl.BlockSpec(memory_space=pltpu.HBM),
        out_shape=jax.ShapeDtypeStruct((exc, 4 * mids, np0 * (nt2 // 2)), f32),
        scratch_shapes=[
            pltpu.VMEM((np1, mids, exc, LANES), f32),
            pltpu.VMEM((np1, mids, exc, LANES), f32),
            pltpu.VMEM((2, np0 // 2, 4 * exc, 2 * LANES), f32),
            pltpu.VMEM((np0 // 2, 4 * mids * exc, LANES), f32),
            pltpu.SemaphoreType.DMA((np0 // 2,)),
        ],
        compiler_params=pltpu.CompilerParams(vmem_limit_bytes=(8 << 20) + np1 * (192 << 10)),
        name="lower",
    )(received, above, *coefs)


def local(
    top_adj,
    level1_adj,
    image_offsets,
    image_weights,
    incidence,
    child_list,
    theta_index_top,
    theta_weight_top,
    phi_weight_top,
    theta_index_mid,
    theta_weight_mid,
    phi_weight_mid,
):
    dev_count = lax.axis_size("dev")
    rhs_count = lax.axis_size("rhs")
    exc, phi_local, top_boxes, top_width = top_adj.shape
    per_dev = top_boxes // dev_count
    nt2 = top_width // 2
    np2 = phi_local * dev_count
    np1 = np2 // 2
    images = image_offsets.shape[0] * rhs_count

    outer, inner = factors(dev_count)
    me = lax.axis_index("dev")
    mids_out, *tops_out = pack(top_adj, level1_adj, dev_count)
    planes = {0: tops_out[0]}
    for k in order(outer):
        planes[k] = lax.ppermute(
            tops_out[k],
            "dev",
            [(s, ((s // inner) ^ k) * inner + s % inner) for s in range(dev_count)],
        )
    received = lax.all_to_all(mids_out, "dev", split_axis=0, concat_axis=0, tiled=True)
    parts = []
    for j in range(inner):
        block = jnp.stack(
            [
                lax.dynamic_index_in_dim(planes[k], (me % inner) ^ j, 0, keepdims=False)
                for k in range(outer)
            ]
        )
        if j:
            block = lax.ppermute(
                block,
                "dev",
                [(s, s // inner * inner + ((s % inner) ^ j)) for s in range(dev_count)],
            )
        parts.append(block)

    own = jnp.concatenate(
        [
            image_offsets.T.astype(jnp.float32),
            image_weights[None] * float(images) ** (-0.5),
        ],
        axis=0,
    )
    images_of = [own]
    for shift in range(1, rhs_count):
        images_of.append(
            lax.ppermute(own, "rhs", [(i, (i + shift) % rhs_count) for i in range(rhs_count)])
        )
    img = jnp.concatenate(images_of + [jnp.zeros((3, LANES - images), jnp.float32)], axis=1)
    where = jnp.stack([lax.axis_index("dev"), lax.axis_index("rhs")]).astype(jnp.int32)
    pw2, pw1, m2, m1, tc, ts, places, phases = tables(
        where,
        child_list,
        phi_weight_top.T,
        phi_weight_mid.T,
        theta_index_top.T,
        theta_weight_top.T,
        theta_index_mid.T,
        theta_weight_mid.T,
        exc,
        nt2,
        per_dev,
    )
    w = lattice(where, incidence.T, img, places, phases, exc, images)
    above = upper(
        parts, (w, pw2, m2), exc, np2, np1, nt2, phi_local, per_dev, outer, inner
    )
    return lower(received, above, (pw1, m1, tc, ts), exc, np1, nt2, phi_local, per_dev)


def order(count):
    steps = list(range(1, count))
    return steps[count // 2 - 1 :] + steps[: count // 2 - 1]


def solution(mesh):
    placed = (
        P("rhs", "dev", None, None),
        P("rhs", "dev", None, None),
        P("rhs", None),
        P("rhs"),
        P(),
        P(),
        P(),
        P(),
        P(),
        P(),
        P(),
        P(),
    )
    return jax.shard_map(
        local, mesh=mesh, in_specs=placed, out_specs=P("rhs", "dev", None), check_vma=False
    )
```

```python
import math

import jax
import jax.numpy as jnp
from jax import lax
from jax.experimental import pallas as pl
from jax.experimental.pallas import tpu as pltpu
from jax.sharding import PartitionSpec as P


PHASE_TOP = 18.85
PHASE_MID = 9.42
LATTICE = 12.57
LANES = 128
MOVED = 1
VMEM = pl.BlockSpec(memory_space=pltpu.VMEM)
SMEM = pl.BlockSpec(memory_space=pltpu.SMEM)


SINE = (3.141592502593994, -5.1677069664001465, 2.5500314235687256, -0.5980451703071594, 0.0772201269865036)
COSINE = (1.0, -4.934802055358887, 4.058709144592285, -1.3352121114730835, 0.23493756353855133, -0.024396715685725212)


def horner(z, factors):
    total = factors[-1]
    for factor in factors[-2::-1]:
        total = total * z + factor
    return total


def sincos(x):
    n = jnp.floor(x + 0.5)
    f = x - n
    z = f * f
    sign = jnp.where((n.astype(jnp.int32) & 1) == 1, -1.0, 1.0)
    return sign * f * horner(z, SINE), sign * horner(z, COSINE)


def directions(shape, theta_count, phi_count):
    rows = lax.broadcasted_iota(jnp.int32, shape, 0).astype(jnp.float32)
    cols = lax.broadcasted_iota(jnp.int32, shape, 1)
    theta = ((cols % theta_count).astype(jnp.float32) + 0.5) / theta_count
    sin_theta, cos_theta = sincos(theta)
    sin_phi, cos_phi = sincos(2.0 / phi_count * rows)
    return cos_phi * sin_theta, sin_phi * sin_theta, cos_theta


def cmul(ar, ai, br, bi):
    return ar * br - ai * bi, ar * bi + ai * br


def loop(count, body):
    if count <= 16:
        for step in range(count):
            body(step)
    else:
        lax.fori_loop(0, count, lambda step, carry: (body(step), carry)[1], 0)


def factors(dev_count):
    inner = 1 << ((dev_count.bit_length() - 1) // 2)
    return dev_count // inner, inner


def pack_kernel(per_dest, outer, inner, a_hbm, l_hbm, mid_hbm, *refs):
    top_hbm = refs[:outer]
    re_ref, im_ref, mid_ref, top_out, mid_out, sems = refs[outer:]
    exc, phi_local, boxes, _ = re_ref.shape
    mid_phi, _ = mid_ref.shape[1:3]
    plane = lax.axis_index("dev") // inner
    arrive = [
        pltpu.make_async_copy(a_hbm.at[:, :, :, pl.ds(0, LANES)], re_ref, sems.at[0]),
        pltpu.make_async_copy(a_hbm.at[:, :, :, pl.ds(LANES, LANES)], im_ref, sems.at[1]),
        pltpu.make_async_copy(l_hbm, mid_ref, sems.at[2]),
    ]
    for copy in arrive:
        copy.start()
    group = 8
    leave = []

    def scatter(source, target):
        count, width, _ = source.shape
        rows = target.reshape(width * count, LANES)

        def one(g):
            for e in range(count):
                start = g * group * count + e
                rows[pl.ds(start, group, stride=count), :] = source[e, pl.ds(g * group, group), :]

        loop(width // group, one)

    def send(source, target):
        copy = pltpu.make_async_copy(source, target, sems.at[3 + len(leave)])
        copy.start()
        leave.append(copy)

    for part, ref in enumerate((re_ref, im_ref)):
        arrive[part].wait()
        for phi in range(phi_local):
            k = phi * 2 + part
            scatter(ref.at[:, phi], top_out.at[k])
            split = top_out.at[k].reshape(boxes // per_dest, per_dest, exc, LANES)
            for other in range(outer):
                for box in range(per_dest):
                    send(
                        split.at[pl.ds((plane ^ other) * inner, inner), box],
                        top_hbm[other].at[:, box * phi_local * 2 + k],
                    )
    arrive[2].wait()
    for phi in range(mid_phi):
        scatter(mid_ref.at[:, phi], mid_out.at[phi])
        split = mid_out.at[phi].reshape(boxes // per_dest, 4 * per_dest, exc, LANES)
        for mid in range(4 * per_dest):
            box, slot = divmod(mid, 4)
            if slot < MOVED:
                tile = (2 * phi_local * per_dest) + (box * MOVED + slot) * mid_phi + phi
                for other in range(outer):
                    send(
                        split.at[pl.ds((plane ^ other) * inner, inner), mid],
                        top_hbm[other].at[:, tile],
                    )
            else:
                tile = (box * (4 - MOVED) + slot - MOVED) * mid_phi + phi
                send(split.at[:, mid], mid_hbm.at[:, tile])
    for copy in leave:
        copy.wait()


def pack(top_adj, level1_adj, dev_count):
    exc, phi_local, boxes, _ = top_adj.shape
    mid_phi, mids = level1_adj.shape[1:3]
    per_dest = boxes // dev_count
    outer, inner = factors(dev_count)
    tops = (phi_local * 2 + MOVED * mid_phi) * per_dest
    rest = (4 - MOVED) * per_dest * mid_phi
    f32 = jnp.float32
    hbm = pl.BlockSpec(memory_space=pltpu.HBM)
    return pl.pallas_call(
        lambda *refs: pack_kernel(per_dest, outer, inner, *refs),
        in_specs=[hbm] * 2,
        out_specs=[hbm] * (1 + outer),
        out_shape=[jax.ShapeDtypeStruct((dev_count, rest, exc, LANES), f32)]
        + [jax.ShapeDtypeStruct((inner, tops, exc, LANES), f32)] * outer,
        scratch_shapes=[
            pltpu.VMEM((exc, phi_local, boxes, LANES), f32),
            pltpu.VMEM((exc, phi_local, boxes, LANES), f32),
            pltpu.VMEM((exc, mid_phi, mids, LANES), f32),
            pltpu.VMEM((phi_local * 2, boxes, exc, LANES), f32),
            pltpu.VMEM((mid_phi, mids, exc, LANES), f32),
            pltpu.SemaphoreType.DMA((3 + outer * tops + rest,)),
        ],
        compiler_params=pltpu.CompilerParams(vmem_limit_bytes=67043328),
        name="pack",
    )(top_adj, level1_adj)


def theta_block(index_ref, weight_ref, columns):
    samples = index_ref.shape[1]
    rows = lax.broadcasted_iota(jnp.int32, (columns, samples), 0)
    total = jnp.zeros((columns, samples), jnp.float32)
    for s in range(3):
        hit = rows == index_ref[s : s + 1, :]
        total = total + jnp.where(hit, weight_ref[s : s + 1, :], 0.0)
    return total


def table_kernel(
    sizes,
    child_ref,
    phi_top_ref,
    phi_mid_ref,
    index_top_ref,
    weight_top_ref,
    index_mid_ref,
    weight_mid_ref,
    inc_ref,
    pw2_ref,
    pw1_ref,
    m2_ref,
    m1_ref,
    tc_ref,
    ts_ref,
    dir_ref,
    ph_ref,
    kk_ref,
    fm_ref,
):
    exc, np2, np1, nt2, per_dev = sizes
    nt1, nt0 = nt2 // 2, nt2 // 4
    first_box = lax.axis_index("dev") * per_dev

    lanes = lax.broadcasted_iota(jnp.int32, (exc, inc_ref.shape[1]), 1)
    rows = lax.broadcasted_iota(jnp.int32, (exc, inc_ref.shape[1]), 0)
    own = lanes == rows + lax.axis_index("rhs") * exc
    for axis in range(2):
        value = jnp.sum(jnp.where(own, inc_ref[axis : axis + 1, :], 0.0), axis=1, keepdims=True)
        kk_ref[axis] = jnp.broadcast_to(value, (exc, LANES))

    def splat_top(p):
        for s in range(3):
            pw2_ref[p * 3 + s] = jnp.full((exc, LANES), phi_top_ref[s, p], jnp.float32)

    def splat_mid(p):
        for s in range(3):
            pw1_ref[p * 3 + s] = jnp.full((exc, LANES), phi_mid_ref[s, p], jnp.float32)

    loop(np2, splat_top)
    loop(np1, splat_mid)

    theta_top = theta_block(index_top_ref, weight_top_ref, nt1)
    theta_mid = theta_block(index_mid_ref, weight_mid_ref, nt0)
    for parts, block, m_ref in ((2, theta_top, m2_ref), (4, theta_mid, m1_ref)):
        high, width = block.shape
        fm_ref[...] = jnp.zeros(fm_ref.shape, jnp.float32)
        for part in range(parts):
            fm_ref[part * high : (part + 1) * high, part * width : (part + 1) * width] = block
        full = jnp.transpose(fm_ref[...])
        coarse = full.astype(jnp.bfloat16)
        m_ref[:, :LANES] = coarse
        m_ref[:, LANES:] = (full - coarse.astype(jnp.float32)).astype(jnp.bfloat16)

    mx, my, mz = directions((np1, LANES), nt1, np1)
    sxs, sxc = sincos(PHASE_MID / math.pi * mx)
    sys_, syc = sincos(PHASE_MID / math.pi * my)
    szs, szc = sincos(PHASE_MID / math.pi * mz)
    lane = lax.broadcasted_iota(jnp.int32, (np1, LANES), 1)
    sign = jnp.where(lane < nt1, -1.0, 1.0)
    for octant in range(4):
        fx = 2.0 * (octant % 2) - 1.0
        fy = 2.0 * (octant // 2) - 1.0
        re, im = cmul(sxc, fx * sxs, syc, fy * sys_)
        re, im = cmul(re, im, szc, -szs)
        tc_ref[octant * np1 : (octant + 1) * np1, :] = re
        ts_ref[octant * np1 : (octant + 1) * np1, :] = im * sign

    ux, uy, uz = directions((np2, LANES), nt2, np2)
    dir_ref[0] = ux
    dir_ref[1] = uy
    axs, axc = sincos(PHASE_TOP / math.pi * ux)
    ays, ayc = sincos(PHASE_TOP / math.pi * uy)
    azs, azc = sincos(PHASE_TOP / math.pi * uz)
    for box in range(per_dev):
        for slot in range(4):
            fx = jnp.float32(0.0)
            fy = jnp.float32(0.0)
            for octant in range(4):
                hit = child_ref[octant, first_box + box] == 4 * (first_box + box) + slot
                fx = fx + jnp.where(hit, jnp.float32(2.0 * (octant % 2) - 1.0), jnp.float32(0.0))
                fy = fy + jnp.where(hit, jnp.float32(2.0 * (octant // 2) - 1.0), jnp.float32(0.0))
            re, im = cmul(axc, fx * axs, ayc, fy * ays)
            re, im = cmul(re, im, azc, -azs)
            ph_ref[box * 8 + slot * 2] = re
            ph_ref[box * 8 + slot * 2 + 1] = im


def lattice_kernel(sizes, inc_ref, img_ref, dir_ref, ph_ref, w_ref, ob_ref):
    exc, np2, images, per_dev = sizes
    half = np2 // 2

    def column(row):
        return jnp.transpose(jnp.broadcast_to(row, (LANES, LANES)))

    image = img_ref[...]
    ox, oy, wt = image[0:1, :], image[1:2, :], image[2:3, :]
    kx, ky = inc_ref[0], inc_ref[1]
    fs, fc = sincos(LATTICE / math.pi * (ox * kx + oy * ky))
    wc = (wt * fc)[:, :images]
    ws = (wt * fs)[:, :images]
    left = jnp.concatenate(
        [
            jnp.concatenate([wc, -ws, wc, -ws], axis=0),
            jnp.concatenate([ws, wc, -ws, -wc], axis=0),
        ],
        axis=1,
    )
    left_high = left.astype(jnp.bfloat16)
    left_low = (left - left_high.astype(jnp.float32)).astype(jnp.bfloat16)
    left_both = jnp.concatenate([left_high, left_low], axis=0)
    ob_ref[0] = column(LATTICE / math.pi * ox)[:images]
    ob_ref[1] = column(LATTICE / math.pi * oy)[:images]

    def sample(p):
        ux_row = dir_ref[0, pl.ds(p, 1), :]
        uy_row = dir_ref[1, pl.ds(p, 1), :]
        sb, cb = sincos(ob_ref[0] * ux_row + ob_ref[1] * uy_row)
        basis = jnp.concatenate([cb, sb], axis=0)
        high = basis.astype(jnp.bfloat16)
        low = (basis - high.astype(jnp.float32)).astype(jnp.bfloat16)
        both = jnp.dot(left_both, high, preferred_element_type=jnp.float32)
        rest = jnp.dot(left_high, low, preferred_element_type=jnp.float32)
        total = both[: 4 * exc] + (both[4 * exc :] + rest)
        for mirror in range(2):
            sr = total[(2 * mirror) * exc : (2 * mirror + 1) * exc]
            si = total[(2 * mirror + 1) * exc : (2 * mirror + 2) * exc]
            q = p + mirror * half
            for tile in range(4 * per_dev):
                pr = ph_ref[2 * tile, pl.ds(q, 1), :]
                pi = ph_ref[2 * tile + 1, pl.ds(q, 1), :]
                re, im = cmul(pr, pi, sr, -si)
                w_ref[q, 2 * tile] = re
                w_ref[q, 2 * tile + 1] = im

    loop(half, sample)


def tables(child, phi_top, phi_mid, tit, twt, tim, twm, inc, exc, nt2, per_dev):
    np2, np1 = phi_top.shape[1], phi_mid.shape[1]
    sizes = (exc, np2, np1, nt2, per_dev)
    f32 = jnp.float32
    return pl.pallas_call(
        lambda *refs: table_kernel(sizes, *refs),
        in_specs=[SMEM] * 3 + [VMEM] * 5,
        out_specs=[VMEM] * 9,
        out_shape=[
            jax.ShapeDtypeStruct((np2 * 3, exc, LANES), f32),
            jax.ShapeDtypeStruct((np1 * 3, exc, LANES), f32),
            jax.ShapeDtypeStruct((2 * nt2, 2 * LANES), jnp.bfloat16),
            jax.ShapeDtypeStruct((2 * nt2, 2 * LANES), jnp.bfloat16),
            jax.ShapeDtypeStruct((4 * np1, LANES), f32),
            jax.ShapeDtypeStruct((4 * np1, LANES), f32),
            jax.ShapeDtypeStruct((2, np2, LANES), f32),
            jax.ShapeDtypeStruct((8 * per_dev, np2, LANES), f32),
            jax.ShapeDtypeStruct((2, exc, LANES), f32),
        ],
        scratch_shapes=[pltpu.VMEM((LANES, 2 * nt2), f32)],
        compiler_params=pltpu.CompilerParams(vmem_limit_bytes=(8 << 20) + np2 * (64 << 10)),
        name="tables",
    )(child, phi_top, phi_mid, tit, twt, tim, twm, inc)


def lattice(inc, img, places, phases, exc, images):
    np2 = places.shape[1]
    per_dev = phases.shape[0] // 8
    f32 = jnp.float32
    return pl.pallas_call(
        lambda *refs: lattice_kernel((exc, np2, images, per_dev), *refs),
        in_specs=[VMEM] * 4,
        out_specs=VMEM,
        out_shape=jax.ShapeDtypeStruct((np2, 8 * per_dev, exc, LANES), f32),
        scratch_shapes=[pltpu.VMEM((2, images, LANES), f32)],
        compiler_params=pltpu.CompilerParams(vmem_limit_bytes=(8 << 20) + np2 * (64 << 10)),
        name="lattice",
    )(inc, img, places, phases)


def split_dot(x, m_ref):
    high = x.astype(jnp.bfloat16)
    low = (x - high.astype(jnp.float32)).astype(jnp.bfloat16)
    wide = jnp.dot(high, m_ref[...], preferred_element_type=jnp.float32)
    rest = jnp.dot(low, m_ref[:, :LANES], preferred_element_type=jnp.float32)
    return wide[:, :LANES] + (wide[:, LANES:] + rest)


def phi_pass(count, contribution, emit, origin=0):
    if count <= 16:
        first = contribution(origin % count)
        here, after = first[1], first[2]
        held = None
        for m in range(1, count):
            new = contribution((m + origin) % count)
            ready = [x + y for x, y in zip(here, new[0])]
            if m == 1:
                held = ready
            else:
                emit((m - 1 + origin) % count, ready)
            here, after = [x + y for x, y in zip(after, new[1])], new[2]
        emit((count - 1 + origin) % count, [x + y for x, y in zip(here, first[0])])
        emit(origin % count, [x + y for x, y in zip(held, after)])
        return

    first = contribution(count - 1)
    second = contribution(0)

    def step(q, carry):
        here, after = carry
        new = contribution(lax.rem(q + 1, count))
        emit(q, [x + y for x, y in zip(here, new[0])])
        return [x + y for x, y in zip(after, new[1])], list(new[2])

    lax.fori_loop(
        0, count, step, ([x + y for x, y in zip(first[2], second[1])], list(second[2]))
    )


def upper_kernel(sizes, *refs):
    exc, _, np1, _, phi_local, per_dev, outer, inner = sizes
    parts = refs[:inner]
    w_ref, pw2_ref, m2_ref, u_ref, r_ref, x_ref = refs[inner:]
    mid_local = phi_local // 2
    tops = phi_local * 2 * per_dev
    me = lax.axis_index("dev")
    for j in range(inner):

        def place(k, j=j):
            source = ((me // inner) ^ k) * inner + ((me % inner) ^ j)
            r_ref[source] = parts[j][k]

        loop(outer, place)

    for box in range(per_dev):

        def top(m, box=box):
            out = [[None] * 8 for _ in range(3)]
            for parity in range(2):
                p = 2 * m + parity
                tile = (box * phi_local + p % phi_local) * 2
                ar = r_ref[p // phi_local, tile]
                ai = r_ref[p // phi_local, tile + 1]
                weights = [pw2_ref[3 * p + s] for s in range(3)]
                for slot in range(4):
                    wr = w_ref[p, box * 8 + slot * 2]
                    wi = w_ref[p, box * 8 + slot * 2 + 1]
                    for c, value in enumerate(cmul(ar, ai, wr, wi)):
                        for s in range(3):
                            term = weights[s] * value
                            k = slot * 2 + c
                            out[s][k] = term if out[s][k] is None else out[s][k] + term
            return out

        chunk = min(np1, 4)

        def theta(part, box=box):
            done = split_dot(x_ref[pl.ds(part * chunk * 4 * exc, chunk * 4 * exc), :], m2_ref)
            for n in range(chunk):
                q = (part * chunk + n + 1) % np1
                for slot in range(4):
                    row = (n * 4 + slot) * exc
                    mid = box * 4 + slot
                    value = done[row : row + exc]
                    if slot < MOVED:
                        tile = tops + (box * MOVED + slot) * mid_local + q % mid_local
                        value = value + r_ref[q // mid_local, tile]
                    u_ref[q, mid] = value

        static = np1 <= 16

        def keep(q, values):
            place = (q + np1 - 1) % np1
            for slot in range(4):
                for c in range(2):
                    x_ref[
                        pl.ds((place * 4 + slot) * exc, exc), c * LANES : (c + 1) * LANES
                    ] = values[slot * 2 + c]
            if static and place % chunk == chunk - 1:
                theta(place // chunk)

        phi_pass(np1, top, keep)
        if not static:
            loop(np1 // chunk, theta)


def lower_kernel(
    sizes, l_ref, u_ref, pw1_ref, m1_ref, tc_ref, ts_ref, o_ref, g_ref, h_ref, y_ref, z_ref, sems
):
    exc, np1, phi_local, per_dev = sizes
    np0 = np1 // 2
    mid_local = phi_local // 2
    mids = 4 * per_dev

    def join(q):
        for mid in range(mids):
            value = u_ref[q, mid]
            box, slot = divmod(mid, 4)
            if slot >= MOVED:
                tile = (box * (4 - MOVED) + slot - MOVED) * mid_local + q % mid_local
                value = value + l_ref[q // mid_local, tile]
            g_ref[q, mid] = value
            h_ref[q, mid] = pltpu.roll(value, LANES // 2, 1)

    loop(np1, join)
    o_rows = o_ref.reshape(exc * 4 * mids, o_ref.shape[2])

    pairs = np0 // 2

    for octant in range(4):
        for box in range(per_dev):

            def middle(m, octant=octant, box=box):
                out = [[None] * 4 for _ in range(3)]
                for parity in range(2):
                    q = 2 * m + parity
                    cosine = tc_ref[pl.ds(octant * np1 + q, 1), :]
                    sine = ts_ref[pl.ds(octant * np1 + q, 1), :]
                    weights = [pw1_ref[3 * q + s] for s in range(3)]
                    for slot in range(4):
                        value = (
                            g_ref[q, box * 4 + slot] * cosine + h_ref[q, box * 4 + slot] * sine
                        )
                        for s in range(3):
                            term = weights[s] * value
                            out[s][slot] = term if out[s][slot] is None else out[s][slot] + term
                return out

            buffer = y_ref.at[octant % 2]

            def keep_low(q, values, buffer=buffer):
                for slot in range(4):
                    buffer[q // 2, pl.ds(slot * exc, exc), pl.ds((q % 2) * LANES, LANES)] = (
                        values[slot]
                    )

            phi_pass(np0, middle, keep_low, 1)

            def finish(part, octant=octant, box=box, buffer=buffer):
                step = min(pairs, 4)
                tile = buffer[pl.ds(part * step, step)].reshape(step * 4 * exc, 2 * LANES)
                done = split_dot(tile, m1_ref)
                for n in range(step):
                    for slot in range(4):
                        k = (box * 4 + slot) * 4 + octant
                        row = (n * 4 + slot) * exc
                        z_ref[part * step + n, pl.ds(k, exc, stride=4 * mids), :] = done[
                            row : row + exc
                        ]

            loop(pairs // min(pairs, 4), finish)

    def leave(pair):
        start = pair * LANES
        lanes = pl.ds(start if isinstance(pair, int) else pl.multiple_of(start, LANES), LANES)
        return pltpu.make_async_copy(z_ref.at[pair], o_rows.at[:, lanes], sems.at[pair])

    loop(pairs, lambda pair: leave(pair).start())
    loop(pairs, lambda pair: leave(pair).wait())


def upper(parts, coefs, exc, np2, np1, nt2, phi_local, per_dev, outer, inner):
    f32 = jnp.float32
    sizes = (exc, np2, np1, nt2, phi_local, per_dev, outer, inner)
    tops = parts[0].shape[1]
    return pl.pallas_call(
        lambda *refs: upper_kernel(sizes, *refs),
        in_specs=[VMEM] * (inner + 3),
        out_specs=VMEM,
        out_shape=jax.ShapeDtypeStruct((np1, 4 * per_dev, exc, LANES), f32),
        scratch_shapes=[
            pltpu.VMEM((outer * inner, tops, exc, LANES), f32),
            pltpu.VMEM((np1 * 4 * exc, 2 * LANES), f32),
        ],
        compiler_params=pltpu.CompilerParams(vmem_limit_bytes=(8 << 20) + np2 * (112 << 10)),
        name="upper",
    )(*parts, *coefs)


def lower(received, above, coefs, exc, np1, nt2, phi_local, per_dev):
    mids = 4 * per_dev
    np0 = np1 // 2
    f32 = jnp.float32
    sizes = (exc, np1, phi_local, per_dev)
    return pl.pallas_call(
        lambda *refs: lower_kernel(sizes, *refs),
        in_specs=[VMEM] * 6,
        out_specs=pl.BlockSpec(memory_space=pltpu.HBM),
        out_shape=jax.ShapeDtypeStruct((exc, 4 * mids, np0 * (nt2 // 2)), f32),
        scratch_shapes=[
            pltpu.VMEM((np1, mids, exc, LANES), f32),
            pltpu.VMEM((np1, mids, exc, LANES), f32),
            pltpu.VMEM((2, np0 // 2, 4 * exc, 2 * LANES), f32),
            pltpu.VMEM((np0 // 2, 4 * mids * exc, LANES), f32),
            pltpu.SemaphoreType.DMA((np0 // 2,)),
        ],
        compiler_params=pltpu.CompilerParams(vmem_limit_bytes=(8 << 20) + np1 * (192 << 10)),
        name="lower",
    )(received, above, *coefs)


def local(
    top_adj,
    level1_adj,
    image_offsets,
    image_weights,
    incidence,
    child_list,
    theta_index_top,
    theta_weight_top,
    phi_weight_top,
    theta_index_mid,
    theta_weight_mid,
    phi_weight_mid,
):
    dev_count = lax.axis_size("dev")
    rhs_count = lax.axis_size("rhs")
    exc, phi_local, top_boxes, top_width = top_adj.shape
    per_dev = top_boxes // dev_count
    nt2 = top_width // 2
    np2 = phi_local * dev_count
    np1 = np2 // 2
    images = image_offsets.shape[0] * rhs_count

    outer, inner = factors(dev_count)
    me = lax.axis_index("dev")
    mids_out, *tops_out = pack(top_adj, level1_adj, dev_count)
    planes = {0: tops_out[0]}
    for k in order(outer):
        planes[k] = lax.ppermute(
            tops_out[k],
            "dev",
            [(s, ((s // inner) ^ k) * inner + s % inner) for s in range(dev_count)],
        )
    received = lax.all_to_all(mids_out, "dev", split_axis=0, concat_axis=0, tiled=True)
    parts = []
    for j in range(inner):
        block = jnp.stack(
            [
                lax.dynamic_index_in_dim(planes[k], (me % inner) ^ j, 0, keepdims=False)
                for k in range(outer)
            ]
        )
        if j:
            block = lax.ppermute(
                block,
                "dev",
                [(s, s // inner * inner + ((s % inner) ^ j)) for s in range(dev_count)],
            )
        parts.append(block)

    own = jnp.concatenate(
        [
            image_offsets.T.astype(jnp.float32),
            image_weights[None] * float(images) ** (-0.5),
        ],
        axis=0,
    )
    images_of = [own]
    for shift in range(1, rhs_count):
        images_of.append(
            lax.ppermute(own, "rhs", [(i, (i + shift) % rhs_count) for i in range(rhs_count)])
        )
    img = jnp.concatenate(images_of + [jnp.zeros((3, LANES - images), jnp.float32)], axis=1)
    pw2, pw1, m2, m1, tc, ts, places, phases, incident = tables(
        child_list.T,
        phi_weight_top.T,
        phi_weight_mid.T,
        theta_index_top.T,
        theta_weight_top.T,
        theta_index_mid.T,
        theta_weight_mid.T,
        incidence.T,
        exc,
        nt2,
        per_dev,
    )
    w = lattice(incident, img, places, phases, exc, images)
    above = upper(
        parts, (w, pw2, m2), exc, np2, np1, nt2, phi_local, per_dev, outer, inner
    )
    return lower(received, above, (pw1, m1, tc, ts), exc, np1, nt2, phi_local, per_dev)


def order(count):
    steps = list(range(1, count))
    return steps[count // 2 - 1 :] + steps[: count // 2 - 1]


def solution(mesh):
    placed = (
        P("rhs", "dev", None, None),
        P("rhs", "dev", None, None),
        P("rhs", None),
        P("rhs"),
        P(),
        P(),
        P(),
        P(),
        P(),
        P(),
        P(),
        P(),
    )
    return jax.shard_map(
        local, mesh=mesh, in_specs=placed, out_specs=P("rhs", "dev", None), check_vma=False
    )
```

```python
import math

import jax
import jax.numpy as jnp
from jax import lax
from jax.experimental import pallas as pl
from jax.experimental.pallas import tpu as pltpu
from jax.sharding import PartitionSpec as P


PHASE_TOP = 18.85
PHASE_MID = 9.42
LATTICE = 12.57
LANES = 128
MOVED = 1
VMEM = pl.BlockSpec(memory_space=pltpu.VMEM)
SMEM = pl.BlockSpec(memory_space=pltpu.SMEM)


SINE = (3.141592502593994, -5.1677069664001465, 2.5500314235687256, -0.5980451703071594, 0.0772201269865036)
COSINE = (1.0, -4.934802055358887, 4.058709144592285, -1.3352121114730835, 0.23493756353855133, -0.024396715685725212)


def horner(z, factors):
    total = factors[-1]
    for factor in factors[-2::-1]:
        total = total * z + factor
    return total


def sincos(x):
    n = jnp.floor(x + 0.5)
    f = x - n
    z = f * f
    sign = jnp.where((n.astype(jnp.int32) & 1) == 1, -1.0, 1.0)
    return sign * f * horner(z, SINE), sign * horner(z, COSINE)


def directions(shape, theta_count, phi_count):
    rows = lax.broadcasted_iota(jnp.int32, shape, 0).astype(jnp.float32)
    cols = lax.broadcasted_iota(jnp.int32, shape, 1)
    theta = ((cols % theta_count).astype(jnp.float32) + 0.5) / theta_count
    sin_theta, cos_theta = sincos(theta)
    sin_phi, cos_phi = sincos(2.0 / phi_count * rows)
    return cos_phi * sin_theta, sin_phi * sin_theta, cos_theta


def cmul(ar, ai, br, bi):
    return ar * br - ai * bi, ar * bi + ai * br


def loop(count, body):
    if count <= 16:
        for step in range(count):
            body(step)
    else:
        lax.fori_loop(0, count, lambda step, carry: (body(step), carry)[1], 0)


def factors(dev_count):
    inner = 1 << ((dev_count.bit_length() - 1) // 2)
    return dev_count // inner, inner


def pack_kernel(per_dest, outer, inner, scale, a_hbm, l_hbm, off_hbm, wt_hbm, mid_hbm, *refs):
    top_hbm = refs[:outer]
    own_hbm, re_ref, im_ref, mid_ref, top_out, mid_out, off_ref, wt_ref, own_ref, sems = refs[outer:]
    exc, phi_local, boxes, _ = re_ref.shape
    mid_phi, _ = mid_ref.shape[1:3]
    plane = lax.axis_index("dev") // inner
    arrive = [
        pltpu.make_async_copy(a_hbm.at[:, :, :, pl.ds(0, LANES)], re_ref, sems.at[0]),
        pltpu.make_async_copy(a_hbm.at[:, :, :, pl.ds(LANES, LANES)], im_ref, sems.at[1]),
        pltpu.make_async_copy(l_hbm, mid_ref, sems.at[2]),
        pltpu.make_async_copy(off_hbm, off_ref, sems.at[3]),
        pltpu.make_async_copy(wt_hbm, wt_ref, sems.at[4]),
    ]
    for copy in arrive:
        copy.start()
    group = 8
    leave = []

    def scatter(source, target):
        count, width, _ = source.shape
        rows = target.reshape(width * count, LANES)

        def one(g):
            for e in range(count):
                start = g * group * count + e
                rows[pl.ds(start, group, stride=count), :] = source[e, pl.ds(g * group, group), :]

        loop(width // group, one)

    def send(source, target):
        copy = pltpu.make_async_copy(source, target, sems.at[5 + len(leave)])
        copy.start()
        leave.append(copy)

    for part, ref in enumerate((re_ref, im_ref)):
        arrive[part].wait()
        for phi in range(phi_local):
            k = phi * 2 + part
            scatter(ref.at[:, phi], top_out.at[k])
            split = top_out.at[k].reshape(boxes // per_dest, per_dest, exc, LANES)
            for other in range(outer):
                for box in range(per_dest):
                    send(
                        split.at[pl.ds((plane ^ other) * inner, inner), box],
                        top_hbm[other].at[:, box * phi_local * 2 + k],
                    )
    arrive[3].wait()
    arrive[4].wait()
    own_ref[0:2, :] = off_ref[...].astype(jnp.float32)
    own_ref[2:3, :] = wt_ref[...] * scale
    send(own_ref, own_hbm)
    arrive[2].wait()
    for phi in range(mid_phi):
        scatter(mid_ref.at[:, phi], mid_out.at[phi])
        split = mid_out.at[phi].reshape(boxes // per_dest, 4 * per_dest, exc, LANES)
        for mid in range(4 * per_dest):
            box, slot = divmod(mid, 4)
            if slot < MOVED:
                tile = (2 * phi_local * per_dest) + (box * MOVED + slot) * mid_phi + phi
                for other in range(outer):
                    send(
                        split.at[pl.ds((plane ^ other) * inner, inner), mid],
                        top_hbm[other].at[:, tile],
                    )
            else:
                tile = (box * (4 - MOVED) + slot - MOVED) * mid_phi + phi
                send(split.at[:, mid], mid_hbm.at[:, tile])
    for copy in leave:
        copy.wait()


def pack(top_adj, level1_adj, offsets, weights, scale, dev_count):
    exc, phi_local, boxes, _ = top_adj.shape
    mid_phi, mids = level1_adj.shape[1:3]
    per_dest = boxes // dev_count
    outer, inner = factors(dev_count)
    tops = (phi_local * 2 + MOVED * mid_phi) * per_dest
    rest = (4 - MOVED) * per_dest * mid_phi
    f32 = jnp.float32
    hbm = pl.BlockSpec(memory_space=pltpu.HBM)
    return pl.pallas_call(
        lambda *refs: pack_kernel(per_dest, outer, inner, scale, *refs),
        in_specs=[hbm] * 4,
        out_specs=[hbm] * (2 + outer),
        out_shape=[jax.ShapeDtypeStruct((dev_count, rest, exc, LANES), f32)]
        + [jax.ShapeDtypeStruct((inner, tops, exc, LANES), f32)] * outer
        + [jax.ShapeDtypeStruct((3, offsets.shape[1]), f32)],
        scratch_shapes=[
            pltpu.VMEM((exc, phi_local, boxes, LANES), f32),
            pltpu.VMEM((exc, phi_local, boxes, LANES), f32),
            pltpu.VMEM((exc, mid_phi, mids, LANES), f32),
            pltpu.VMEM((phi_local * 2, boxes, exc, LANES), f32),
            pltpu.VMEM((mid_phi, mids, exc, LANES), f32),
            pltpu.VMEM(offsets.shape, jnp.int32),
            pltpu.VMEM(weights.shape, f32),
            pltpu.VMEM((3, offsets.shape[1]), f32),
            pltpu.SemaphoreType.DMA((6 + outer * tops + rest,)),
        ],
        compiler_params=pltpu.CompilerParams(vmem_limit_bytes=67043328),
        name="pack",
    )(top_adj, level1_adj, offsets, weights)


def theta_block(index_ref, weight_ref, columns):
    samples = index_ref.shape[1]
    rows = lax.broadcasted_iota(jnp.int32, (columns, samples), 0)
    total = jnp.zeros((columns, samples), jnp.float32)
    for s in range(3):
        hit = rows == index_ref[s : s + 1, :]
        total = total + jnp.where(hit, weight_ref[s : s + 1, :], 0.0)
    return total


def table_kernel(
    sizes,
    child_ref,
    phi_top_ref,
    phi_mid_ref,
    index_top_ref,
    weight_top_ref,
    index_mid_ref,
    weight_mid_ref,
    inc_ref,
    pw2_ref,
    pw1_ref,
    m2_ref,
    m1_ref,
    tc_ref,
    ts_ref,
    dir_ref,
    ph_ref,
    kk_ref,
    fm_ref,
):
    exc, np2, np1, nt2, per_dev = sizes
    nt1, nt0 = nt2 // 2, nt2 // 4
    first_box = lax.axis_index("dev") * per_dev

    lanes = lax.broadcasted_iota(jnp.int32, (exc, inc_ref.shape[1]), 1)
    rows = lax.broadcasted_iota(jnp.int32, (exc, inc_ref.shape[1]), 0)
    own = lanes == rows + lax.axis_index("rhs") * exc
    for axis in range(2):
        value = jnp.sum(jnp.where(own, inc_ref[axis : axis + 1, :], 0.0), axis=1, keepdims=True)
        kk_ref[axis] = jnp.broadcast_to(value, (exc, LANES))

    def splat_top(p):
        for s in range(3):
            pw2_ref[p * 3 + s] = jnp.full((exc, LANES), phi_top_ref[s, p], jnp.float32)

    def splat_mid(p):
        for s in range(3):
            pw1_ref[p * 3 + s] = jnp.full((exc, LANES), phi_mid_ref[s, p], jnp.float32)

    loop(np2, splat_top)
    loop(np1, splat_mid)

    theta_top = theta_block(index_top_ref, weight_top_ref, nt1)
    theta_mid = theta_block(index_mid_ref, weight_mid_ref, nt0)
    for parts, block, m_ref in ((2, theta_top, m2_ref), (4, theta_mid, m1_ref)):
        high, width = block.shape
        fm_ref[...] = jnp.zeros(fm_ref.shape, jnp.float32)
        for part in range(parts):
            fm_ref[part * high : (part + 1) * high, part * width : (part + 1) * width] = block
        full = jnp.transpose(fm_ref[...])
        coarse = full.astype(jnp.bfloat16)
        m_ref[:, :LANES] = coarse
        m_ref[:, LANES:] = (full - coarse.astype(jnp.float32)).astype(jnp.bfloat16)

    mx, my, mz = directions((np1, LANES), nt1, np1)
    sxs, sxc = sincos(PHASE_MID / math.pi * mx)
    sys_, syc = sincos(PHASE_MID / math.pi * my)
    szs, szc = sincos(PHASE_MID / math.pi * mz)
    lane = lax.broadcasted_iota(jnp.int32, (np1, LANES), 1)
    sign = jnp.where(lane < nt1, -1.0, 1.0)
    for octant in range(4):
        fx = 2.0 * (octant % 2) - 1.0
        fy = 2.0 * (octant // 2) - 1.0
        re, im = cmul(sxc, fx * sxs, syc, fy * sys_)
        re, im = cmul(re, im, szc, -szs)
        tc_ref[octant * np1 : (octant + 1) * np1, :] = re
        ts_ref[octant * np1 : (octant + 1) * np1, :] = im * sign

    ux, uy, uz = directions((np2, LANES), nt2, np2)
    dir_ref[0] = ux
    dir_ref[1] = uy
    axs, axc = sincos(PHASE_TOP / math.pi * ux)
    ays, ayc = sincos(PHASE_TOP / math.pi * uy)
    azs, azc = sincos(PHASE_TOP / math.pi * uz)
    for box in range(per_dev):
        for slot in range(4):
            fx = jnp.float32(0.0)
            fy = jnp.float32(0.0)
            for octant in range(4):
                hit = child_ref[octant, first_box + box] == 4 * (first_box + box) + slot
                fx = fx + jnp.where(hit, jnp.float32(2.0 * (octant % 2) - 1.0), jnp.float32(0.0))
                fy = fy + jnp.where(hit, jnp.float32(2.0 * (octant // 2) - 1.0), jnp.float32(0.0))
            re, im = cmul(axc, fx * axs, ayc, fy * ays)
            re, im = cmul(re, im, azc, -azs)
            ph_ref[box * 8 + slot * 2] = re
            ph_ref[box * 8 + slot * 2 + 1] = im


def lattice_kernel(sizes, inc_ref, img_ref, dir_ref, ph_ref, w_ref, ob_ref):
    exc, np2, images, per_dev = sizes
    half = np2 // 2

    def column(row):
        return jnp.transpose(jnp.broadcast_to(row, (LANES, LANES)))

    image = img_ref[...]
    ox, oy, wt = image[0:1, :], image[1:2, :], image[2:3, :]
    kx, ky = inc_ref[0], inc_ref[1]
    fs, fc = sincos(LATTICE / math.pi * (ox * kx + oy * ky))
    wc = (wt * fc)[:, :images]
    ws = (wt * fs)[:, :images]
    left = jnp.concatenate(
        [
            jnp.concatenate([wc, -ws, wc, -ws], axis=0),
            jnp.concatenate([ws, wc, -ws, -wc], axis=0),
        ],
        axis=1,
    )
    left_high = left.astype(jnp.bfloat16)
    left_low = (left - left_high.astype(jnp.float32)).astype(jnp.bfloat16)
    left_both = jnp.concatenate([left_high, left_low], axis=0)
    ob_ref[0] = column(LATTICE / math.pi * ox)[:images]
    ob_ref[1] = column(LATTICE / math.pi * oy)[:images]

    def sample(p):
        ux_row = dir_ref[0, pl.ds(p, 1), :]
        uy_row = dir_ref[1, pl.ds(p, 1), :]
        sb, cb = sincos(ob_ref[0] * ux_row + ob_ref[1] * uy_row)
        basis = jnp.concatenate([cb, sb], axis=0)
        high = basis.astype(jnp.bfloat16)
        low = (basis - high.astype(jnp.float32)).astype(jnp.bfloat16)
        both = jnp.dot(left_both, high, preferred_element_type=jnp.float32)
        rest = jnp.dot(left_high, low, preferred_element_type=jnp.float32)
        total = both[: 4 * exc] + (both[4 * exc :] + rest)
        for mirror in range(2):
            sr = total[(2 * mirror) * exc : (2 * mirror + 1) * exc]
            si = total[(2 * mirror + 1) * exc : (2 * mirror + 2) * exc]
            q = p + mirror * half
            for tile in range(4 * per_dev):
                pr = ph_ref[2 * tile, pl.ds(q, 1), :]
                pi = ph_ref[2 * tile + 1, pl.ds(q, 1), :]
                re, im = cmul(pr, pi, sr, -si)
                w_ref[q, 2 * tile] = re
                w_ref[q, 2 * tile + 1] = im

    loop(half, sample)


def tables(child, phi_top, phi_mid, tit, twt, tim, twm, inc, exc, nt2, per_dev):
    np2, np1 = phi_top.shape[1], phi_mid.shape[1]
    sizes = (exc, np2, np1, nt2, per_dev)
    f32 = jnp.float32
    return pl.pallas_call(
        lambda *refs: table_kernel(sizes, *refs),
        in_specs=[SMEM] * 3 + [VMEM] * 5,
        out_specs=[VMEM] * 9,
        out_shape=[
            jax.ShapeDtypeStruct((np2 * 3, exc, LANES), f32),
            jax.ShapeDtypeStruct((np1 * 3, exc, LANES), f32),
            jax.ShapeDtypeStruct((2 * nt2, 2 * LANES), jnp.bfloat16),
            jax.ShapeDtypeStruct((2 * nt2, 2 * LANES), jnp.bfloat16),
            jax.ShapeDtypeStruct((4 * np1, LANES), f32),
            jax.ShapeDtypeStruct((4 * np1, LANES), f32),
            jax.ShapeDtypeStruct((2, np2, LANES), f32),
            jax.ShapeDtypeStruct((8 * per_dev, np2, LANES), f32),
            jax.ShapeDtypeStruct((2, exc, LANES), f32),
        ],
        scratch_shapes=[pltpu.VMEM((LANES, 2 * nt2), f32)],
        compiler_params=pltpu.CompilerParams(vmem_limit_bytes=(8 << 20) + np2 * (64 << 10)),
        name="tables",
    )(child, phi_top, phi_mid, tit, twt, tim, twm, inc)


def lattice(inc, img, places, phases, exc, images):
    np2 = places.shape[1]
    per_dev = phases.shape[0] // 8
    f32 = jnp.float32
    return pl.pallas_call(
        lambda *refs: lattice_kernel((exc, np2, images, per_dev), *refs),
        in_specs=[VMEM] * 4,
        out_specs=VMEM,
        out_shape=jax.ShapeDtypeStruct((np2, 8 * per_dev, exc, LANES), f32),
        scratch_shapes=[pltpu.VMEM((2, images, LANES), f32)],
        compiler_params=pltpu.CompilerParams(vmem_limit_bytes=(8 << 20) + np2 * (64 << 10)),
        name="lattice",
    )(inc, img, places, phases)


def split_dot(x, m_ref):
    high = x.astype(jnp.bfloat16)
    low = (x - high.astype(jnp.float32)).astype(jnp.bfloat16)
    wide = jnp.dot(high, m_ref[...], preferred_element_type=jnp.float32)
    rest = jnp.dot(low, m_ref[:, :LANES], preferred_element_type=jnp.float32)
    return wide[:, :LANES] + (wide[:, LANES:] + rest)


def phi_pass(count, contribution, emit, origin=0):
    if count <= 16:
        first = contribution(origin % count)
        here, after = first[1], first[2]
        held = None
        for m in range(1, count):
            new = contribution((m + origin) % count)
            ready = [x + y for x, y in zip(here, new[0])]
            if m == 1:
                held = ready
            else:
                emit((m - 1 + origin) % count, ready)
            here, after = [x + y for x, y in zip(after, new[1])], new[2]
        emit((count - 1 + origin) % count, [x + y for x, y in zip(here, first[0])])
        emit(origin % count, [x + y for x, y in zip(held, after)])
        return

    first = contribution(count - 1)
    second = contribution(0)

    def step(q, carry):
        here, after = carry
        new = contribution(lax.rem(q + 1, count))
        emit(q, [x + y for x, y in zip(here, new[0])])
        return [x + y for x, y in zip(after, new[1])], list(new[2])

    lax.fori_loop(
        0, count, step, ([x + y for x, y in zip(first[2], second[1])], list(second[2]))
    )


def upper_kernel(sizes, *refs):
    exc, _, np1, _, phi_local, per_dev, outer, inner = sizes
    parts = refs[:inner]
    w_ref, pw2_ref, m2_ref, u_ref, r_ref, x_ref = refs[inner:]
    mid_local = phi_local // 2
    tops = phi_local * 2 * per_dev
    me = lax.axis_index("dev")
    for j in range(inner):

        def place(k, j=j):
            source = ((me // inner) ^ k) * inner + ((me % inner) ^ j)
            r_ref[source] = parts[j][k]

        loop(outer, place)

    for box in range(per_dev):

        def top(m, box=box):
            out = [[None] * 8 for _ in range(3)]
            for parity in range(2):
                p = 2 * m + parity
                tile = (box * phi_local + p % phi_local) * 2
                ar = r_ref[p // phi_local, tile]
                ai = r_ref[p // phi_local, tile + 1]
                weights = [pw2_ref[3 * p + s] for s in range(3)]
                for slot in range(4):
                    wr = w_ref[p, box * 8 + slot * 2]
                    wi = w_ref[p, box * 8 + slot * 2 + 1]
                    for c, value in enumerate(cmul(ar, ai, wr, wi)):
                        for s in range(3):
                            term = weights[s] * value
                            k = slot * 2 + c
                            out[s][k] = term if out[s][k] is None else out[s][k] + term
            return out

        chunk = min(np1, 4)

        def theta(part, box=box):
            done = split_dot(x_ref[pl.ds(part * chunk * 4 * exc, chunk * 4 * exc), :], m2_ref)
            for n in range(chunk):
                q = (part * chunk + n + 1) % np1
                for slot in range(4):
                    row = (n * 4 + slot) * exc
                    mid = box * 4 + slot
                    value = done[row : row + exc]
                    if slot < MOVED:
                        tile = tops + (box * MOVED + slot) * mid_local + q % mid_local
                        value = value + r_ref[q // mid_local, tile]
                    u_ref[q, mid] = value

        static = np1 <= 16

        def keep(q, values):
            place = (q + np1 - 1) % np1
            for slot in range(4):
                for c in range(2):
                    x_ref[
                        pl.ds((place * 4 + slot) * exc, exc), c * LANES : (c + 1) * LANES
                    ] = values[slot * 2 + c]
            if static and place % chunk == chunk - 1:
                theta(place // chunk)

        phi_pass(np1, top, keep)
        if not static:
            loop(np1 // chunk, theta)


def lower_kernel(
    sizes, l_ref, u_ref, pw1_ref, m1_ref, tc_ref, ts_ref, o_ref, g_ref, h_ref, y_ref, z_ref, sems
):
    exc, np1, phi_local, per_dev = sizes
    np0 = np1 // 2
    mid_local = phi_local // 2
    mids = 4 * per_dev

    def join(q):
        for mid in range(mids):
            value = u_ref[q, mid]
            box, slot = divmod(mid, 4)
            if slot >= MOVED:
                tile = (box * (4 - MOVED) + slot - MOVED) * mid_local + q % mid_local
                value = value + l_ref[q // mid_local, tile]
            g_ref[q, mid] = value
            h_ref[q, mid] = pltpu.roll(value, LANES // 2, 1)

    loop(np1, join)
    o_rows = o_ref.reshape(exc * 4 * mids, o_ref.shape[2])

    pairs = np0 // 2

    for octant in range(4):
        for box in range(per_dev):

            def middle(m, octant=octant, box=box):
                out = [[None] * 4 for _ in range(3)]
                for parity in range(2):
                    q = 2 * m + parity
                    cosine = tc_ref[pl.ds(octant * np1 + q, 1), :]
                    sine = ts_ref[pl.ds(octant * np1 + q, 1), :]
                    weights = [pw1_ref[3 * q + s] for s in range(3)]
                    for slot in range(4):
                        value = (
                            g_ref[q, box * 4 + slot] * cosine + h_ref[q, box * 4 + slot] * sine
                        )
                        for s in range(3):
                            term = weights[s] * value
                            out[s][slot] = term if out[s][slot] is None else out[s][slot] + term
                return out

            buffer = y_ref.at[octant % 2]

            def keep_low(q, values, buffer=buffer):
                for slot in range(4):
                    buffer[q // 2, pl.ds(slot * exc, exc), pl.ds((q % 2) * LANES, LANES)] = (
                        values[slot]
                    )

            phi_pass(np0, middle, keep_low, 1)

            def finish(part, octant=octant, box=box, buffer=buffer):
                step = min(pairs, 4)
                tile = buffer[pl.ds(part * step, step)].reshape(step * 4 * exc, 2 * LANES)
                done = split_dot(tile, m1_ref)
                for n in range(step):
                    for slot in range(4):
                        k = (box * 4 + slot) * 4 + octant
                        row = (n * 4 + slot) * exc
                        z_ref[part * step + n, pl.ds(k, exc, stride=4 * mids), :] = done[
                            row : row + exc
                        ]

            loop(pairs // min(pairs, 4), finish)

    def leave(pair):
        start = pair * LANES
        lanes = pl.ds(start if isinstance(pair, int) else pl.multiple_of(start, LANES), LANES)
        return pltpu.make_async_copy(z_ref.at[pair], o_rows.at[:, lanes], sems.at[pair])

    loop(pairs, lambda pair: leave(pair).start())
    loop(pairs, lambda pair: leave(pair).wait())


def upper(parts, coefs, exc, np2, np1, nt2, phi_local, per_dev, outer, inner):
    f32 = jnp.float32
    sizes = (exc, np2, np1, nt2, phi_local, per_dev, outer, inner)
    tops = parts[0].shape[1]
    return pl.pallas_call(
        lambda *refs: upper_kernel(sizes, *refs),
        in_specs=[VMEM] * (inner + 3),
        out_specs=VMEM,
        out_shape=jax.ShapeDtypeStruct((np1, 4 * per_dev, exc, LANES), f32),
        scratch_shapes=[
            pltpu.VMEM((outer * inner, tops, exc, LANES), f32),
            pltpu.VMEM((np1 * 4 * exc, 2 * LANES), f32),
        ],
        compiler_params=pltpu.CompilerParams(vmem_limit_bytes=(8 << 20) + np2 * (112 << 10)),
        name="upper",
    )(*parts, *coefs)


def lower(received, above, coefs, exc, np1, nt2, phi_local, per_dev):
    mids = 4 * per_dev
    np0 = np1 // 2
    f32 = jnp.float32
    sizes = (exc, np1, phi_local, per_dev)
    return pl.pallas_call(
        lambda *refs: lower_kernel(sizes, *refs),
        in_specs=[VMEM] * 6,
        out_specs=pl.BlockSpec(memory_space=pltpu.HBM),
        out_shape=jax.ShapeDtypeStruct((exc, 4 * mids, np0 * (nt2 // 2)), f32),
        scratch_shapes=[
            pltpu.VMEM((np1, mids, exc, LANES), f32),
            pltpu.VMEM((np1, mids, exc, LANES), f32),
            pltpu.VMEM((2, np0 // 2, 4 * exc, 2 * LANES), f32),
            pltpu.VMEM((np0 // 2, 4 * mids * exc, LANES), f32),
            pltpu.SemaphoreType.DMA((np0 // 2,)),
        ],
        compiler_params=pltpu.CompilerParams(vmem_limit_bytes=(8 << 20) + np1 * (192 << 10)),
        name="lower",
    )(received, above, *coefs)


def local(
    top_adj,
    level1_adj,
    image_offsets,
    image_weights,
    incidence,
    child_list,
    theta_index_top,
    theta_weight_top,
    phi_weight_top,
    theta_index_mid,
    theta_weight_mid,
    phi_weight_mid,
):
    dev_count = lax.axis_size("dev")
    rhs_count = lax.axis_size("rhs")
    exc, phi_local, top_boxes, top_width = top_adj.shape
    per_dev = top_boxes // dev_count
    nt2 = top_width // 2
    np2 = phi_local * dev_count
    np1 = np2 // 2
    images = image_offsets.shape[0] * rhs_count

    outer, inner = factors(dev_count)
    me = lax.axis_index("dev")
    mids_out, *tops_out, own = pack(
        top_adj,
        level1_adj,
        image_offsets.T,
        image_weights[None],
        float(images) ** (-0.5),
        dev_count,
    )
    planes = {0: tops_out[0]}
    for k in order(outer):
        planes[k] = lax.ppermute(
            tops_out[k],
            "dev",
            [(s, ((s // inner) ^ k) * inner + s % inner) for s in range(dev_count)],
        )
    received = lax.all_to_all(mids_out, "dev", split_axis=0, concat_axis=0, tiled=True)
    parts = []
    for j in range(inner):
        block = jnp.stack(
            [
                lax.dynamic_index_in_dim(planes[k], (me % inner) ^ j, 0, keepdims=False)
                for k in range(outer)
            ]
        )
        if j:
            block = lax.ppermute(
                block,
                "dev",
                [(s, s // inner * inner + ((s % inner) ^ j)) for s in range(dev_count)],
            )
        parts.append(block)

    images_of = [own]
    for shift in range(1, rhs_count):
        images_of.append(
            lax.ppermute(own, "rhs", [(i, (i + shift) % rhs_count) for i in range(rhs_count)])
        )
    img = jnp.concatenate(images_of + [jnp.zeros((3, LANES - images), jnp.float32)], axis=1)
    pw2, pw1, m2, m1, tc, ts, places, phases, incident = tables(
        child_list.T,
        phi_weight_top.T,
        phi_weight_mid.T,
        theta_index_top.T,
        theta_weight_top.T,
        theta_index_mid.T,
        theta_weight_mid.T,
        incidence.T,
        exc,
        nt2,
        per_dev,
    )
    w = lattice(incident, img, places, phases, exc, images)
    above = upper(
        parts, (w, pw2, m2), exc, np2, np1, nt2, phi_local, per_dev, outer, inner
    )
    return lower(received, above, (pw1, m1, tc, ts), exc, np1, nt2, phi_local, per_dev)


def order(count):
    steps = list(range(1, count))
    return steps[count // 2 - 1 :] + steps[: count // 2 - 1]


def solution(mesh):
    placed = (
        P("rhs", "dev", None, None),
        P("rhs", "dev", None, None),
        P("rhs", None),
        P("rhs"),
        P(),
        P(),
        P(),
        P(),
        P(),
        P(),
        P(),
        P(),
    )
    return jax.shard_map(
        local, mesh=mesh, in_specs=placed, out_specs=P("rhs", "dev", None), check_vma=False
    )
```
